512 devices in a mesh: dp: 128 (over y, z, core), mp: 4 (over x).
Axes of the slice: x: 4, y: 8, z: 8, core: 2. Of those that a mesh axis runs over, the one named last changes fastest.
Arguments:
- public_input_activations: bfloat16 [128, 112, 8192], P('dp', None, 'mp')
- public_output_cotangents: bfloat16 [128, 112, 8192], P('dp', None, 'mp')
- public_token_lengths: int32 [128], P('dp'), may hold values from 28 to 112, as said below
- private_input_activations: bfloat16 [512, 112, 8192], P('dp', None, 'mp')
- private_output_cotangents: bfloat16 [512, 112, 8192], P('dp', None, 'mp')
- private_token_lengths: int32 [512], P('dp'), may hold values from 28 to 112, as said below
- adapter_down_matrix: bfloat16 [8192, 16], P('mp'), may hold values from -0.0625 to 0.0625
- adapter_up_matrix: bfloat16 [16, 8192], P(None, 'mp'), may hold values from -0.0625 to 0.0625
- embedding_coefficient_noise: float32 [128], replicated, may hold values from -6 to 6
- residual_down_noise: float32 [4, 32768], P('mp', 'dp'), may hold values from -6 to 6
- residual_up_noise: float32 [4, 32768], P('mp', 'dp'), may hold values from -6 to 6
Outputs:
- update_down: float32 [4, 32768], P('mp', 'dp')
- update_up: float32 [4, 32768], P('mp', 'dp')
The draws below stay inside these ranges and needn't reach their ends.
Inputs may be any that keep to these rules, and one draw needn't show every extreme that they name: `public_token_lengths`: each example has between 28 and 112 live tokens at the start of its slots. `private_token_lengths`: each example has between 28 and 112 live tokens at the start of its slots.
All inputs are finite; a program needn't handle non-finite values.
Results may differ from the reference program's by a relative error of at most 0.0028.
Values may be sent and summed in bfloat16 or wider, within the bound.
A program may use at most 64 MiB of HBM per device.

```python
import math
import jax
import jax.numpy as jnp
from jax import lax

MODEL_WIDTH = 8192
ADAPTER_RANK = 16
TOKEN_SLOTS = 112
PRIV = 512
PUB = 128
PSHARD = 256
N_MP = 4


def feature_profile(key):
    inner = jax.random.fold_in(key, 7)
    first_key, second_key, third_key = jax.random.split(inner, 3)
    ramp = 1.0 + 2.0 * jnp.arange(MODEL_WIDTH, dtype=jnp.float32) / (MODEL_WIDTH - 1)
    rough = jax.random.uniform(first_key, (MODEL_WIDTH,), jnp.float32, 0.7, 1.4)
    heavy_count = max(PSHARD // ADAPTER_RANK, 1)
    heavy_start = jax.random.randint(third_key, (), 0, MODEL_WIDTH // heavy_count, dtype=jnp.int32) * heavy_count
    feature_index = jnp.arange(MODEL_WIDTH, dtype=jnp.int32)
    heavy_mask = jnp.logical_and(feature_index >= heavy_start, feature_index < heavy_start + heavy_count)
    boost = jnp.where(heavy_mask, 6.0, 1.0).astype(jnp.float32)
    centre = jax.random.normal(second_key, (MODEL_WIDTH,), jnp.float32)
    return (ramp * rough * boost, centre)


def cluster_centres(key, public, example_total_count):
    input_centres = jax.random.normal(jax.random.fold_in(key, 31), (PUB, MODEL_WIDTH), jnp.float32)
    output_centres = jax.random.normal(jax.random.fold_in(key, 32), (PUB, MODEL_WIDTH), jnp.float32)
    if public:
        cluster = jnp.arange(PUB, dtype=jnp.int32)
        weight_key = jax.random.fold_in(key, 41)
    else:
        cluster = jax.random.randint(jax.random.fold_in(key, 33), (example_total_count,), 0, PUB, dtype=jnp.int32)
        weight_key = jax.random.fold_in(key, 42)
    strength = jnp.exp(jax.random.uniform(weight_key, (example_total_count,), jnp.float32, math.log(0.25), math.log(2.0)))
    return (input_centres[cluster] * strength[:, None], output_centres[cluster])


def draw_activations(key, salt, example_total_count, public):
    feature_scale, centre = feature_profile(key)
    input_cluster, output_cluster = cluster_centres(key, public, example_total_count)
    noise_key, example_key = jax.random.split(jax.random.fold_in(key, salt), 2)
    fresh = jax.random.normal(noise_key, (example_total_count, TOKEN_SLOTS, MODEL_WIDTH), jnp.float32)
    spread = jnp.log(3.0)
    example_scale = jnp.exp(jax.random.uniform(example_key, (example_total_count, 1, 1), jnp.float32, 0.0, 1.0) * spread)
    return (example_scale * feature_scale * (centre + input_cluster[:, None, :] + fresh)).astype(jnp.bfloat16)


def draw_cotangents(key, salt, example_total_count, public):
    input_cluster, output_cluster = cluster_centres(key, public, example_total_count)
    noise_key = jax.random.fold_in(key, salt)
    fresh = jax.random.normal(noise_key, (example_total_count, TOKEN_SLOTS, MODEL_WIDTH), jnp.float32)
    cluster_gain = 3.0 / math.sqrt(TOKEN_SLOTS)
    return (fresh + cluster_gain * output_cluster[:, None, :]).astype(jnp.bfloat16)


def draw_token_lengths(key, salt, example_total_count):
    values = jax.random.randint(jax.random.fold_in(key, salt), (example_total_count,), TOKEN_SLOTS // 4, TOKEN_SLOTS + 1, dtype=jnp.int32)
    return values.at[0].set(TOKEN_SLOTS).at[1].set(TOKEN_SLOTS // 4)


def draw_public_input_activations(key, part):
    return draw_activations(key, 11, PUB, True)


def draw_private_input_activations(key, part):
    return draw_activations(key, 13, PRIV, False)


def draw_public_output_cotangents(key, part):
    return draw_cotangents(key, 15, PUB, True)


def draw_private_output_cotangents(key, part):
    return draw_cotangents(key, 17, PRIV, False)


def draw_public_token_lengths(key, part):
    return draw_token_lengths(key, 21, PUB)


def draw_private_token_lengths(key, part):
    return draw_token_lengths(key, 22, PRIV)


def levels(rng, shape, cuts, low, largest):
    gain, own = 1.0, jax.random.fold_in(rng, 6)
    for dim, shards_of in cuts:
        heights = jnp.exp(jax.random.uniform(jax.random.fold_in(own, dim), (shards_of,), jnp.float32, low / len(cuts), largest / len(cuts)))
        gain = gain * jnp.repeat(heights, shape[dim] // shards_of).reshape([-1 if axis == dim else 1 for axis in range(len(shape))])
    return gain


def centred(rng, extent, scale, reach, shards=(), kind=jnp.bfloat16):
    values = jax.random.normal(rng, extent, jnp.float32) * scale
    if len(shards) > 0:
        values = levels(rng, extent, shards, -0.22, 0.18) * values
    return jnp.clip(values, min=-reach, max=reach).astype(kind)


def setup_inputs(seed: int = 0) -> dict:
    streams_of = jax.random.split(jax.random.key(seed), 12)
    public_input_activations = draw_public_input_activations(jax.random.fold_in(streams_of[11], 71), 0)
    public_output_cotangents = draw_public_output_cotangents(jax.random.fold_in(streams_of[11], 71), 0)
    public_token_lengths = draw_public_token_lengths(jax.random.fold_in(streams_of[11], 71), 0)
    private_input_activations = draw_private_input_activations(jax.random.fold_in(streams_of[11], 71), 0)
    private_output_cotangents = draw_private_output_cotangents(jax.random.fold_in(streams_of[11], 71), 0)
    private_token_lengths = draw_private_token_lengths(jax.random.fold_in(streams_of[11], 71), 0)
    adapter_down_matrix = centred(streams_of[6], (MODEL_WIDTH, ADAPTER_RANK), MODEL_WIDTH ** -0.5, 0.0625, ((0, 4),))
    adapter_up_matrix = centred(streams_of[7], (ADAPTER_RANK, MODEL_WIDTH), MODEL_WIDTH ** -0.5, 0.0625, ((1, 4),))
    embedding_coefficient_noise = centred(streams_of[8], (PUB,), 1.0, 6.0, (), jnp.float32)
    residual_down_noise = centred(streams_of[9], (N_MP, MODEL_WIDTH // N_MP * ADAPTER_RANK), 1.0, 6.0, ((0, 4), (1, 128)), jnp.float32)
    residual_up_noise = centred(streams_of[10], (N_MP, MODEL_WIDTH // N_MP * ADAPTER_RANK), 1.0, 6.0, ((0, 4), (1, 128)), jnp.float32)
    return dict(public_input_activations=public_input_activations, public_output_cotangents=public_output_cotangents, public_token_lengths=public_token_lengths, private_input_activations=private_input_activations, private_output_cotangents=private_output_cotangents, private_token_lengths=private_token_lengths, adapter_down_matrix=adapter_down_matrix, adapter_up_matrix=adapter_up_matrix, embedding_coefficient_noise=embedding_coefficient_noise, residual_down_noise=residual_down_noise, residual_up_noise=residual_up_noise)


CLIP_COEF = 0.5
CLIP_RESIDUAL = 0.7
SIGMA_COEF = 1.0
SIGMA_RESIDUAL = 0.04
PRECISE = lax.Precision.HIGHEST

def per_example_gradients(input_activations, output_cotangents, token_lengths, adapter_down_matrix, adapter_up_matrix):
    example_total_count = input_activations.shape[0]
    block_width = MODEL_WIDTH // N_MP
    projected_gradients = jnp.dot(input_activations.reshape(example_total_count * TOKEN_SLOTS, MODEL_WIDTH).astype(jnp.float32), adapter_down_matrix.astype(jnp.float32), preferred_element_type=jnp.float32).reshape(example_total_count, TOKEN_SLOTS, ADAPTER_RANK)
    reconstructed_gradients = jnp.dot(output_cotangents.reshape(example_total_count * TOKEN_SLOTS, MODEL_WIDTH).astype(jnp.float32), adapter_up_matrix.T.astype(jnp.float32), preferred_element_type=jnp.float32).reshape(example_total_count, TOKEN_SLOTS, ADAPTER_RANK)
    positions = lax.broadcasted_iota(jnp.int32, (example_total_count, TOKEN_SLOTS), 1)
    live_mask = (positions < token_lengths[:, None]).astype(jnp.float32)[:, :, None]
    projected_live = lax.optimization_barrier((projected_gradients * live_mask).astype(jnp.bfloat16)).astype(jnp.float32)
    returned_live = lax.optimization_barrier((reconstructed_gradients * live_mask).astype(jnp.bfloat16)).astype(jnp.float32)

    def one_block(block_index):
        start = (block_index * block_width).astype(jnp.int32)
        input_block = lax.dynamic_slice_in_dim(input_activations, start, block_width, 2).astype(jnp.float32)
        cotangent_block = lax.dynamic_slice_in_dim(output_cotangents, start, block_width, 2).astype(jnp.float32)
        grad_down = jnp.einsum('etd,etr->edr', input_block, returned_live, precision=PRECISE)
        grad_up = jnp.einsum('etr,eto->ero', projected_live, cotangent_block, precision=PRECISE)
        joined = jnp.concatenate([grad_down.reshape(example_total_count, block_width * ADAPTER_RANK), grad_up.reshape(example_total_count, ADAPTER_RANK * block_width)], axis=1)
        return joined.astype(jnp.bfloat16)
    return lax.map(one_block, jnp.arange(N_MP, dtype=jnp.int32))

def lower_solve(factor, right_side, backward):
    return lax.linalg.triangular_solve(factor, right_side, left_side=True, lower=True, transpose_a=backward)

def reference(public_input_activations, public_output_cotangents, public_token_lengths, private_input_activations, private_output_cotangents, private_token_lengths, adapter_down_matrix, adapter_up_matrix, embedding_coefficient_noise, residual_down_noise, residual_up_noise):
    public_group = per_example_gradients(public_input_activations, public_output_cotangents, public_token_lengths, adapter_down_matrix, adapter_up_matrix)
    private_group = per_example_gradients(private_input_activations, private_output_cotangents, private_token_lengths, adapter_down_matrix, adapter_up_matrix)
    public_flat = public_group.transpose(1, 0, 2).reshape(PUB, -1)
    private_flat = private_group.transpose(1, 0, 2).reshape(PRIV, -1)
    gram_matrix = jnp.dot(public_flat.astype(jnp.float32), public_flat.T.astype(jnp.float32), preferred_element_type=jnp.float32)
    cross_terms = jnp.dot(public_flat.astype(jnp.float32), private_flat.T.astype(jnp.float32), preferred_element_type=jnp.float32)
    factor = jnp.linalg.cholesky(gram_matrix)
    norm_scale = jnp.mean(jnp.sqrt(jnp.diagonal(gram_matrix)))
    coefficient_limit = CLIP_COEF * norm_scale
    residual_limit = CLIP_RESIDUAL * norm_scale
    coeffs = lower_solve(factor, cross_terms, False)
    weights = lower_solve(factor, coeffs, True)

    def residual_block(running, block_index):
        public_block = public_group[block_index].astype(jnp.float32)
        private_block = private_group[block_index].astype(jnp.float32)
        residual = private_block - jnp.dot(weights.T, public_block, precision=PRECISE)
        return (running + lax.optimization_barrier(jnp.sum(residual * residual, axis=1)), block_index)
    residual_squares = lax.scan(residual_block, jnp.zeros((PRIV,), jnp.float32), jnp.arange(N_MP, dtype=jnp.int32))[0]
    coefficient_norm = jnp.sqrt(lax.optimization_barrier(jnp.sum(coeffs * coeffs, axis=0)))
    keep_coefficient = coefficient_limit / jnp.maximum(coefficient_norm, coefficient_limit)
    keep_residual = residual_limit / jnp.maximum(jnp.sqrt(residual_squares), residual_limit)
    target = jnp.dot(coeffs, keep_coefficient - keep_residual, precision=PRECISE) + SIGMA_COEF * coefficient_limit * embedding_coefficient_noise
    anchor = lower_solve(factor, target[:, None], True)[:, 0]

    def update_block(block_index):
        public_block = public_group[block_index].astype(jnp.float32)
        private_block = private_group[block_index].astype(jnp.float32)
        return jnp.dot(anchor, public_block, precision=PRECISE) + jnp.dot(keep_residual, private_block, precision=PRECISE)
    update = lax.map(update_block, jnp.arange(N_MP, dtype=jnp.int32))
    noise_whole = jnp.concatenate([residual_down_noise, residual_up_noise], axis=1)
    update_gain = 1.0 / math.sqrt(PRIV * TOKEN_SLOTS)
    update = (update + SIGMA_RESIDUAL * residual_limit * noise_whole) * update_gain
    split_point = MODEL_WIDTH // N_MP * ADAPTER_RANK
    return (update[:, :split_point], update[:, split_point:])
```

```python
import math

import jax
import jax.numpy as jnp
from jax import lax
from jax.experimental import pallas as pl
from jax.experimental.pallas import tpu as pltpu
from jax.sharding import PartitionSpec as P

CLIP_COEF = 0.5
CLIP_RESIDUAL = 0.7
SIGMA_COEF = 1.0
SIGMA_RESIDUAL = 0.04
PRECISE = lax.Precision.HIGHEST
BF, F32 = jnp.bfloat16, jnp.float32
NX, NY, NZ, NC = 4, 8, 8, 2
NS = NZ * NC
E = 5
T = 112
W = 2048
R = 16
MESH = pl.DeviceIdType.MESH


def lane_blocks(rows):
    rows = list(rows)
    block = lax.broadcasted_iota(jnp.int32, rows[0].shape, rows[0].ndim - 1) // R
    axis = rows[0].ndim - 1
    for bit in (1, 2, 4):
        low = (block & bit) == 0
        fresh = list(rows)
        for i in range(8):
            if i & bit:
                continue
            j = i | bit
            fresh[i] = jnp.where(low, rows[i], pltpu.roll(rows[j], R * bit, axis))
            fresh[j] = jnp.where(low, pltpu.roll(rows[i], 128 - R * bit, axis), rows[j])
        rows = fresh
    return rows


def body_kernel(
    pub_len, priv_len, pub_in, pub_cot, priv_in, priv_cot, down_mat, up_mat,
    total_ref, grads_ref,
    proj, proj_in, d1s, d1r, u1s, u1r, d2s, d2r, u2s, u2r,
    mine, rc, m1, ry, m2, rz, m3, rx, m4,
    sx, gx, sd1, gd1, su1, gu1, sd2, gd2, su2, gu2,
    sc, gc, sy, gy, sz, gz, sxx, gxx, say, gay, sac, gac,
):
    x = lax.axis_index("mp")
    d = lax.axis_index("dp")
    y = d // NS
    s = d % NS
    z = s // NC
    c = s % NC

    def at(yy, ss, xx):
        return (yy * NS + ss, xx)

    xs = [lax.rem(x + k, NX) for k in range(NX)]
    ys = [lax.rem(y + k, NY) for k in range(NY)]
    ss = [lax.rem(s + k, NS) for k in range(NS)]
    zs = [lax.rem(z + k, NZ) for k in range(NZ)]
    other = 1 - c

    barrier = pltpu.get_barrier_semaphore()
    for k in range(1, NX):
        pl.semaphore_signal(barrier, inc=1, device_id=at(y, s, xs[k]), device_id_type=MESH)
    for k in range(1, NY):
        pl.semaphore_signal(barrier, inc=1, device_id=at(ys[k], s, x), device_id_type=MESH)
    for k in range(1, NS):
        pl.semaphore_signal(barrier, inc=1, device_id=at(y, ss[k], x), device_id_type=MESH)

    def send(src, dst, ssem, rsem, who):
        copy = pltpu.make_async_remote_copy(
            src_ref=src, dst_ref=dst, send_sem=ssem, recv_sem=rsem, device_id=who, device_id_type=MESH
        )
        copy.start()
        return copy

    def partial(inputs, cotangents):
        p = jnp.dot(inputs, down_mat[...], preferred_element_type=F32)
        r = lax.dot_general(cotangents, up_mat[...], (((1,), (1,)), ((), ())), preferred_element_type=F32)
        return jnp.concatenate([p, r, jnp.zeros((p.shape[0], 128 - 2 * R), F32)], axis=1)

    blocks = []
    for e in range(E):
        ins = pub_in[0] if e == 0 else priv_in[e - 1]
        cots = pub_cot[0] if e == 0 else priv_cot[e - 1]
        both = partial(ins, cots)
        both = jnp.concatenate([both, jnp.zeros((128 - T, 128), F32)], axis=0)
        proj[:, 128 * e : 128 * (e + 1)] = both.T[: 2 * R]
    proj_in[x] = proj[...]

    pl.semaphore_wait(barrier, NX + NY + NS - 3)
    copies = [send(proj, proj_in.at[x], sx.at[k], gx.at[k], at(y, s, xs[k])) for k in range(1, NX)]
    for copy in copies:
        copy.wait()
    total = proj_in[0] + proj_in[1] + proj_in[2] + proj_in[3]
    token = lax.broadcasted_iota(jnp.int32, (2 * R, 128), 1)
    row = lax.broadcasted_iota(jnp.int32, (R, R), 0)
    col = lax.broadcasted_iota(jnp.int32, (R, R), 1)
    order = (col == 2 * (row % 8) + row // 8).astype(BF)
    for e in range(E):
        length = pub_len[0] if e == 0 else priv_len[e - 1]
        live = (total[:, 128 * e : 128 * (e + 1)] * (token < length).astype(F32)).astype(BF)
        pt = jnp.dot(order, live[:R], preferred_element_type=F32).astype(BF)
        rt = live[R:]
        ins = pub_in[0] if e == 0 else priv_in[e - 1]
        cots = pub_cot[0] if e == 0 else priv_cot[e - 1]
        gd = jnp.dot(rt[:, :T], ins, preferred_element_type=F32).astype(BF)
        for k in range(NY):
            d1s[k, R * e : R * (e + 1), :] = gd[:, 256 * k : 256 * (k + 1)]
        gu = jnp.dot(pt[:, :T], cots, preferred_element_type=F32)
        for k in range(NS):
            hi, lo = k // 8, k % 8
            rows = gu[8 * hi : 8 * hi + 8]
            pair = jnp.concatenate([rows[:, 256 * lo : 256 * lo + 128], rows[:, 256 * lo + 128 : 256 * lo + 256]], axis=0)
            u1s[k, R * e : R * (e + 1), :] = pair.astype(BF)

    d1 = [send(d1s.at[ys[k]], d1r.at[y], sd1.at[k], gd1.at[k], at(ys[k], s, x)) for k in range(1, NY)]
    u1 = [send(u1s.at[ss[k]], u1r.at[s], su1.at[k], gu1.at[k], at(y, ss[k], x)) for k in range(1, NS)]
    d1r[y] = d1s[y]
    u1r[s] = u1s[s]

    for copy in d1:
        copy.wait()
    for e in range(E):
        for hi in range(2):
            tiles = [d1r[k, R * e : R * (e + 1), 128 * hi : 128 * (hi + 1)].astype(F32) for k in range(NY)]
            halves = []
            for rh in range(2):
                cube = jnp.stack([t[8 * rh : 8 * rh + 8] for t in tiles], axis=0)
                cube = jnp.swapaxes(cube, 0, 1)
                halves.append(lane_blocks([cube[i] for i in range(8)]))
            for lo in range(8):
                pair = jnp.concatenate([halves[0][lo], halves[1][lo]], axis=0)
                d2s[8 * hi + lo, R * e : R * (e + 1), :] = pair.astype(BF)
    d2 = [send(d2s.at[ss[k]], d2r.at[s], sd2.at[k], gd2.at[k], at(y, ss[k], x)) for k in range(1, NS)]
    d2r[s] = d2s[s]

    def flip(ref):
        for e in range(E):
            tiles = [ref[k, R * e : R * (e + 1), :].astype(F32) for k in range(NS)]
            for h in range(2):
                cube = jnp.stack([t[8 * h : 8 * h + 8] for t in tiles], axis=0)
                yield e, h, jnp.swapaxes(cube, 0, 1)

    for copy in u1:
        copy.wait()
    for e, h, cube in flip(u1r):
        u2s[:, R * (2 * e + h) : R * (2 * e + h + 1), :] = cube.astype(BF)
    u2 = [send(u2s.at[ys[k]], u2r.at[y], su2.at[k], gu2.at[k], at(ys[k], s, x)) for k in range(1, NY)]
    u2r[y] = u2s[y]

    for copy in d2:
        copy.wait()
    for e, h, cube in flip(d2r):
        grads_ref[128 * e : 128 * (e + 1), 128 * h : 128 * (h + 1)] = cube.astype(BF).reshape(128, 128)
    for copy in u2:
        copy.wait()
    for e in range(E):
        for h in range(2):
            k = 2 * e + h
            grads_ref[128 * e : 128 * (e + 1), 256 + 128 * h : 256 + 128 * (h + 1)] = u2r[
                :, R * k : R * (k + 1), :
            ].reshape(128, 128)

    whole = grads_ref[...]
    product = lax.dot_general(whole[:128], whole, (((1,), (1,)), ((), ())), preferred_element_type=F32)
    wide = whole[128:].astype(F32)
    norms = lax.dot_general(
        jnp.ones((8, 512), F32), wide * wide, (((1,), (1,)), ((), ())), preferred_element_type=F32, precision=PRECISE
    )
    lane = lax.broadcasted_iota(jnp.int32, (8, 128), 1)
    sub = lax.broadcasted_iota(jnp.int32, (8, 128), 0)
    top = product[:8, :128]
    for i in range(8):
        piece = norms[:, 128 * (i // 2) : 128 * (i // 2) + 128]
        if i % 2 == 0:
            piece = pltpu.roll(piece, 64, 1)
        top = jnp.where((sub == i) & (lane >= 64), piece, top)
    mine[...] = product.reshape(2, 8, 8, 640)
    mine[0, 0, :, :128] = top

    copy = send(mine.at[other], rc, sc.at[0], gc.at[0], at(y, z * NC + other, x))
    copy.wait()
    m1[...] = mine[c] + rc[...]
    copies = [send(m1.at[ys[k]], ry.at[y], sy.at[k], gy.at[k], at(ys[k], s, x)) for k in range(1, NY)]
    ry[y] = m1[y]
    for copy in copies:
        copy.wait()
    m2[...] = sum([ry[k] for k in range(1, NY)], ry[0])
    copies = [send(m2, rz.at[z], sz.at[k], gz.at[k], at(y, zs[k] * NC + c, x)) for k in range(1, NZ)]
    rz[z] = m2[...]
    for copy in copies:
        copy.wait()
    m3[...] = sum([rz[k] for k in range(1, NZ)], rz[0])
    copies = [send(m3, rx.at[x], sxx.at[k], gxx.at[k], at(y, s, xs[k])) for k in range(1, NX)]
    rx[x] = m3[...]
    for copy in copies:
        copy.wait()
    m4[...] = sum([rx[k] for k in range(1, NX)], rx[0])
    copies = [send(m4, total_ref.at[c, y], say.at[k], gay.at[k], at(ys[k], s, x)) for k in range(1, NY)]
    total_ref[c, y] = m4[...]
    for copy in copies:
        copy.wait()
    copy = send(total_ref.at[c], total_ref.at[c], sac.at[0], gac.at[0], at(y, z * NC + other, x))
    copy.wait()


def exchange(*args):
    dma = pltpu.SemaphoreType.DMA
    v = pltpu.VMEM
    vm = pl.BlockSpec(memory_space=pltpu.VMEM)
    sm = pl.BlockSpec(memory_space=pltpu.SMEM)
    sems = []
    for n in (NX, NY, NS, NS, NY, 1, NY, NZ, NX, NY, 1):
        sems += [dma((n,)), dma((n,))]
    return pl.pallas_call(
        body_kernel,
        out_shape=(jax.ShapeDtypeStruct((2, 8, 8, 640), F32), jax.ShapeDtypeStruct((640, 512), BF)),
        in_specs=[sm, sm] + [vm] * 6,
        out_specs=(vm, vm),
        scratch_shapes=[
            v((2 * R, 640), F32), v((NX, 2 * R, 640), F32),
            v((NY, 80, 256), BF), v((NY, 80, 256), BF),
            v((NS, 80, 128), BF), v((NS, 80, 128), BF),
            v((NS, 80, 128), BF), v((NS, 80, 128), BF),
            v((NY, 160, 128), BF), v((NY, 160, 128), BF),
            v((2, 8, 8, 640), F32), v((8, 8, 640), F32), v((8, 8, 640), F32), v((NY, 8, 640), F32),
            v((8, 640), F32), v((NZ, 8, 640), F32), v((8, 640), F32), v((NX, 8, 640), F32), v((8, 640), F32),
        ] + sems,
        compiler_params=pltpu.CompilerParams(collective_id=0, has_side_effects=True, vmem_limit_bytes=48 * 1024 * 1024),
    )(*args)


def lower_solve(factor, right_side, backward):
    return lax.linalg.triangular_solve(
        factor, right_side, left_side=True, lower=True, transpose_a=backward
    )


def body(
    public_input_activations,
    public_output_cotangents,
    public_token_lengths,
    private_input_activations,
    private_output_cotangents,
    private_token_lengths,
    adapter_down_matrix,
    adapter_up_matrix,
    embedding_coefficient_noise,
    residual_down_noise,
    residual_up_noise,
):
    total, grads = exchange(
        public_token_lengths, private_token_lengths,
        public_input_activations, public_output_cotangents,
        private_input_activations, private_output_cotangents,
        adapter_down_matrix, adapter_up_matrix,
    )
    total = total.reshape(128, 640)
    squares = total[:8, 64:128].reshape(512)
    low = jnp.tril(total[:, :128])
    gram_matrix = low + jnp.tril(low, -1).T
    cross_terms = total[:, 128:]
    factor = jnp.linalg.cholesky(gram_matrix, symmetrize_input=False)
    norm_scale = jnp.mean(jnp.sqrt(jnp.diagonal(gram_matrix)))
    coefficient_limit = CLIP_COEF * norm_scale
    residual_limit = CLIP_RESIDUAL * norm_scale
    coeffs = lower_solve(factor, cross_terms, False)
    coefficient_squares = jnp.sum(coeffs * coeffs, axis=0)
    residual_squares = jnp.maximum(squares - coefficient_squares, 0.0)
    keep_coefficient = coefficient_limit / jnp.maximum(jnp.sqrt(coefficient_squares), coefficient_limit)
    keep_residual = residual_limit / jnp.maximum(jnp.sqrt(residual_squares), residual_limit)
    correction = jnp.dot(coeffs, keep_coefficient - keep_residual, precision=PRECISE)
    target = correction + SIGMA_COEF * coefficient_limit * embedding_coefficient_noise
    anchor = lower_solve(factor, target[:, None], True)[:, 0]
    weights = jnp.concatenate([anchor, keep_residual])
    update = jnp.sum(weights[:, None] * grads.astype(F32), axis=0)
    down = update[:256].reshape(16, 16).T.reshape(256)
    up = update[256:]
    update_gain = 1.0 / math.sqrt(512 * T)
    down = (down + SIGMA_RESIDUAL * residual_limit * residual_down_noise[0]) * update_gain
    up = (up + SIGMA_RESIDUAL * residual_limit * residual_up_noise[0]) * update_gain
    return (down[None], up[None])


def solution(mesh):
    placed = (
        P("dp", None, "mp"),
        P("dp", None, "mp"),
        P("dp"),
        P("dp", None, "mp"),
        P("dp", None, "mp"),
        P("dp"),
        P("mp", None),
        P(None, "mp"),
        P(),
        P("mp", "dp"),
        P("mp", "dp"),
    )
    return jax.shard_map(
        body, mesh=mesh, in_specs=placed, out_specs=(P("mp", "dp"), P("mp", "dp")), check_vma=False
    )
```

```python
import math

import jax
import jax.numpy as jnp
from jax import lax
from jax.experimental import pallas as pl
from jax.experimental.pallas import tpu as pltpu
from jax.sharding import PartitionSpec as P

CLIP_COEF = 0.5
CLIP_RESIDUAL = 0.7
SIGMA_COEF = 1.0
SIGMA_RESIDUAL = 0.04
PRECISE = lax.Precision.HIGHEST
BF, F32 = jnp.bfloat16, jnp.float32
NX, NY, NZ, NC = 4, 8, 8, 2
NS = NZ * NC
E = 5
T = 112
W = 2048
R = 16
MESH = pl.DeviceIdType.MESH


def lane_blocks(rows):
    rows = list(rows)
    block = lax.broadcasted_iota(jnp.int32, rows[0].shape, rows[0].ndim - 1) // R
    axis = rows[0].ndim - 1
    for bit in (1, 2, 4):
        low = (block & bit) == 0
        fresh = list(rows)
        for i in range(8):
            if i & bit:
                continue
            j = i | bit
            fresh[i] = jnp.where(low, rows[i], pltpu.roll(rows[j], R * bit, axis))
            fresh[j] = jnp.where(low, pltpu.roll(rows[i], 128 - R * bit, axis), rows[j])
        rows = fresh
    return rows


def spread_lane(v, j):
    return jnp.broadcast_to(v[:, j : j + 1], v.shape)


def spread_row(v, i):
    return jnp.broadcast_to(v[i : i + 1], v.shape)


def tree(terms):
    terms = list(terms)
    while len(terms) > 1:
        terms = [sum(terms[i + 1 : i + 2], terms[i]) for i in range(0, len(terms), 2)]
    return terms[0]


def stacked(rows, sub):
    for bit in (1, 2, 4):
        odd = (sub & bit) != 0
        rows = [jnp.where(odd, rows[i + 1], rows[i]) for i in range(0, len(rows), 2)]
    return rows[0]


def inverse_factor(g):
    g = list(g)
    shape = (8, 128)
    sub = lax.broadcasted_iota(jnp.int32, shape, 0)
    lane = lax.broadcasted_iota(jnp.int32, shape, 1)
    right = [(lane == sub + 8 * k).astype(F32) for k in range(16)]
    zero = jnp.zeros(shape, F32)
    out = []
    for k in range(16):
        top, edge = g[k], right[k]
        cols = [spread_lane(top, 8 * k + j) for j in range(8)]
        a = {(i, j): spread_row(cols[j], i) for j in range(8) for i in range(j, 8)}
        inv = {}
        low = {}
        for j in range(8):
            p = a[j, j]
            r = lax.rsqrt(p)
            r = r * (1.5 - 0.5 * p * r * r)
            inv[j, j] = r
            for i in range(j + 1, 8):
                low[i, j] = a[i, j] * r
            for m in range(j + 1, 8):
                for i in range(m, 8):
                    a[i, m] = a[i, m] - low[i, j] * low[m, j]
            for i in range(j):
                inv[j, i] = -r * tree([low[j, m] * inv[m, i] for m in range(i, j)])
        top_rows = [spread_row(top, j) for j in range(8)]
        edge_rows = [spread_row(edge, j) for j in range(8)]
        inv_cols = [stacked([inv.get((i, j), zero) for i in range(8)], sub) for j in range(8)]
        edge = tree([inv_cols[j] * edge_rows[j] for j in range(8)])
        out.append(edge)
        if k == 15:
            break
        top = tree([inv_cols[j] * top_rows[j] for j in range(8)])
        top_rows = [spread_row(top, j) for j in range(8)]
        edge_rows = [spread_row(edge, j) for j in range(8)]
        for m in range(k + 1, 16):
            raw = [spread_lane(g[m], 8 * k + j) for j in range(8)]
            factors = [tree([raw[i] * inv[j, i] for i in range(j + 1)]) for j in range(8)]
            g[m] = g[m] - tree([factors[j] * top_rows[j] for j in range(8)])
            right[m] = right[m] - tree([factors[j] * edge_rows[j] for j in range(8)])
    return jnp.concatenate(out, axis=0)


def split(v):
    high = v.astype(BF)
    rest = v - high.astype(F32)
    middle = rest.astype(BF)
    return high, middle, (rest - middle.astype(F32)).astype(BF)


def exact_rows(row, matrix):
    terms = [t.astype(F32) for t in split(row)]
    terms = jnp.concatenate(terms + [jnp.zeros((5, row.shape[1]), F32)], axis=0).astype(BF)
    out = jnp.dot(terms, matrix, preferred_element_type=F32)
    return out[0:1] + out[1:2] + out[2:3]


def body_kernel(
    pub_len, priv_len, pub_in_hbm, pub_cot_hbm, priv_in_hbm, priv_cot_hbm, down_hbm, up_hbm,
    coef_noise, down_noise, up_noise,
    down_out, up_out,
    ins, cots, down_mat, up_mat, load_sem,
    total_ref, grads_ref, swap,
    proj, proj_in, d1s, d1r, u1s, u1r, d2s, d2r, u2s, u2r,
    mine, rc, m1, ry, m2, rz, m3, rx, m4,
    sx, gx, sd1, gd1, su1, gu1, sd2, gd2, su2, gu2,
    sc, gc, sy, gy, sz, gz, sxx, gxx, say, gay, sac, gac,
):
    loads = [
        pltpu.make_async_copy(src, dst, load_sem.at[k])
        for k, (src, dst) in enumerate(
            [(down_hbm, down_mat), (up_hbm, up_mat), (pub_in_hbm.at[0], ins.at[0]), (pub_cot_hbm.at[0], cots.at[0])]
            + [
                pair
                for e in range(4)
                for pair in ((priv_in_hbm.at[e], ins.at[e + 1]), (priv_cot_hbm.at[e], cots.at[e + 1]))
            ]
        )
    ]
    for load in loads:
        load.start()
    x = lax.axis_index("mp")
    d = lax.axis_index("dp")
    y = d // NS
    s = d % NS
    z = s // NC
    c = s % NC

    def at(yy, ss, xx):
        return (yy * NS + ss, xx)

    xs = [lax.rem(x + k, NX) for k in range(NX)]
    ys = [lax.rem(y + k, NY) for k in range(NY)]
    ss = [lax.rem(s + k, NS) for k in range(NS)]
    zs = [lax.rem(z + k, NZ) for k in range(NZ)]
    other = 1 - c

    barrier = pltpu.get_barrier_semaphore()
    for k in range(1, NX):
        pl.semaphore_signal(barrier, inc=1, device_id=at(y, s, xs[k]), device_id_type=MESH)
    for k in range(1, NY):
        pl.semaphore_signal(barrier, inc=1, device_id=at(ys[k], s, x), device_id_type=MESH)
    for k in range(1, NS):
        pl.semaphore_signal(barrier, inc=1, device_id=at(y, ss[k], x), device_id_type=MESH)

    def send(src, dst, ssem, rsem, who):
        copy = pltpu.make_async_remote_copy(
            src_ref=src, dst_ref=dst, send_sem=ssem, recv_sem=rsem, device_id=who, device_id_type=MESH
        )
        copy.start()
        return copy

    loads[0].wait()
    loads[1].wait()
    for e in range(E):
        loads[2 + 2 * e].wait()
        loads[3 + 2 * e].wait()
        p = lax.dot_general(ins[e], down_mat[...], (((1,), (1,)), ((), ())), preferred_element_type=F32)
        r = lax.dot_general(cots[e], up_mat[...], (((1,), (1,)), ((), ())), preferred_element_type=F32)
        both = jnp.concatenate([p, r, jnp.zeros((T, 128 - 2 * R), F32)], axis=1)
        both = jnp.concatenate([both, jnp.zeros((128 - T, 128), F32)], axis=0)
        proj[:, 128 * e : 128 * (e + 1)] = both.T[: 2 * R]
    proj_in[x] = proj[...]

    before = lax.broadcasted_iota(jnp.int32, (256, 256), 0)
    after = lax.broadcasted_iota(jnp.int32, (256, 256), 1)
    swap[...] = ((before % R == after // R) & (before // R == after % R)).astype(BF)

    pl.semaphore_wait(barrier, NX + NY + NS - 3)
    copies = [send(proj, proj_in.at[x], sx.at[k], gx.at[k], at(y, s, xs[k])) for k in range(1, NX)]
    for copy in copies:
        copy.wait()
    total = proj_in[0] + proj_in[1] + proj_in[2] + proj_in[3]
    token = lax.broadcasted_iota(jnp.int32, (2 * R, 128), 1)
    row = lax.broadcasted_iota(jnp.int32, (R, R), 0)
    col = lax.broadcasted_iota(jnp.int32, (R, R), 1)
    order = (col == 2 * (row % 8) + row // 8).astype(BF)
    for e in range(E):
        length = pub_len[0] if e == 0 else priv_len[e - 1]
        live = (total[:, 128 * e : 128 * (e + 1)] * (token < length).astype(F32)).astype(BF)
        pt = jnp.dot(order, live[:R], preferred_element_type=F32).astype(BF)
        rt = live[R:]
        gd = jnp.dot(rt[:, :T], ins[e], preferred_element_type=F32).astype(BF)
        for k in range(NY):
            d1s[k, R * e : R * (e + 1), :] = gd[:, 256 * k : 256 * (k + 1)]
        gu = jnp.dot(pt[:, :T], cots[e], preferred_element_type=F32)
        for k in range(NS):
            hi, lo = k // 8, k % 8
            rows = gu[8 * hi : 8 * hi + 8]
            pair = jnp.concatenate([rows[:, 256 * lo : 256 * lo + 128], rows[:, 256 * lo + 128 : 256 * lo + 256]], axis=0)
            u1s[k, R * e : R * (e + 1), :] = pair.astype(BF)

    d1 = [send(d1s.at[ys[k]], d1r.at[y], sd1.at[k], gd1.at[k], at(ys[k], s, x)) for k in range(1, NY)]
    u1 = [send(u1s.at[ss[k]], u1r.at[s], su1.at[k], gu1.at[k], at(y, ss[k], x)) for k in range(1, NS)]
    d1r[y] = d1s[y]
    u1r[s] = u1s[s]

    for copy in d1:
        copy.wait()
    for e in range(E):
        for hi in range(2):
            tiles = [d1r[k, R * e : R * (e + 1), 128 * hi : 128 * (hi + 1)].astype(F32) for k in range(NY)]
            halves = []
            for rh in range(2):
                cube = jnp.stack([t[8 * rh : 8 * rh + 8] for t in tiles], axis=0)
                cube = jnp.swapaxes(cube, 0, 1)
                halves.append(lane_blocks([cube[i] for i in range(8)]))
            for lo in range(8):
                pair = jnp.concatenate([halves[0][lo], halves[1][lo]], axis=0)
                d2s[8 * hi + lo, R * e : R * (e + 1), :] = pair.astype(BF)
    d2 = [send(d2s.at[ss[k]], d2r.at[s], sd2.at[k], gd2.at[k], at(y, ss[k], x)) for k in range(1, NS)]
    d2r[s] = d2s[s]

    def flip(ref):
        for e in range(E):
            tiles = [ref[k, R * e : R * (e + 1), :].astype(F32) for k in range(NS)]
            for h in range(2):
                cube = jnp.stack([t[8 * h : 8 * h + 8] for t in tiles], axis=0)
                yield e, h, jnp.swapaxes(cube, 0, 1)

    for copy in u1:
        copy.wait()
    for e, h, cube in flip(u1r):
        u2s[:, R * (2 * e + h) : R * (2 * e + h + 1), :] = cube.astype(BF)
    u2 = [send(u2s.at[ys[k]], u2r.at[y], su2.at[k], gu2.at[k], at(ys[k], s, x)) for k in range(1, NY)]
    u2r[y] = u2s[y]

    for copy in d2:
        copy.wait()
    for e, h, cube in flip(d2r):
        grads_ref[128 * e : 128 * (e + 1), 128 * h : 128 * (h + 1)] = cube.astype(BF).reshape(128, 128)
    for copy in u2:
        copy.wait()
    for e in range(E):
        for h in range(2):
            k = 2 * e + h
            grads_ref[128 * e : 128 * (e + 1), 256 + 128 * h : 256 + 128 * (h + 1)] = u2r[
                :, R * k : R * (k + 1), :
            ].reshape(128, 128)

    whole = grads_ref[...]
    product = lax.dot_general(whole[:128], whole, (((1,), (1,)), ((), ())), preferred_element_type=F32)
    wide = whole[128:].astype(F32)
    wide = wide * wide
    high = wide.astype(BF)
    rest = (wide - high.astype(F32)).astype(BF)
    ones = jnp.ones((8, 512), BF)
    norms = lax.dot_general(ones, high, (((1,), (1,)), ((), ())), preferred_element_type=F32)
    norms = norms + lax.dot_general(ones, rest, (((1,), (1,)), ((), ())), preferred_element_type=F32)
    lane = lax.broadcasted_iota(jnp.int32, (8, 128), 1)
    sub = lax.broadcasted_iota(jnp.int32, (8, 128), 0)
    top = product[:8, :128]
    for i in range(8):
        piece = norms[:, 128 * (i // 2) : 128 * (i // 2) + 128]
        if i % 2 == 0:
            piece = pltpu.roll(piece, 64, 1)
        top = jnp.where((sub == i) & (lane >= 64), piece, top)
    mine[...] = product.reshape(2, 8, 8, 640)
    mine[0, 0, :, :128] = top

    copy = send(mine.at[other], rc, sc.at[0], gc.at[0], at(y, z * NC + other, x))
    copy.wait()
    m1[...] = mine[c] + rc[...]
    copies = [send(m1.at[ys[k]], ry.at[y], sy.at[k], gy.at[k], at(ys[k], s, x)) for k in range(1, NY)]
    ry[y] = m1[y]
    for copy in copies:
        copy.wait()
    m2[...] = sum([ry[k] for k in range(1, NY)], ry[0])
    copies = [send(m2, rz.at[z], sz.at[k], gz.at[k], at(y, zs[k] * NC + c, x)) for k in range(1, NZ)]
    rz[z] = m2[...]
    for copy in copies:
        copy.wait()
    m3[...] = sum([rz[k] for k in range(1, NZ)], rz[0])
    copies = [send(m3, rx.at[x], sxx.at[k], gxx.at[k], at(y, s, xs[k])) for k in range(1, NX)]
    rx[x] = m3[...]
    for copy in copies:
        copy.wait()
    m4[...] = sum([rx[k] for k in range(1, NX)], rx[0])
    copies = [send(m4, total_ref.at[c, y], say.at[k], gay.at[k], at(ys[k], s, x)) for k in range(1, NY)]
    total_ref[c, y] = m4[...]
    for copy in copies:
        copy.wait()
    copy = send(total_ref.at[c], total_ref.at[c], sac.at[0], gac.at[0], at(y, z * NC + other, x))
    copy.wait()

    both = total_ref[...].reshape(128, 640)
    square, cross = both[:, :128], both[:, 128:]
    sub = lax.broadcasted_iota(jnp.int32, (128, 128), 0)
    lane = lax.broadcasted_iota(jnp.int32, (128, 128), 1)
    gram = jnp.where(lane > sub, square.T, square)
    diagonal = lane == sub
    norm_scale = jnp.mean(
        jnp.sqrt(jnp.sum(jnp.where(diagonal, gram, 0.0), axis=0, keepdims=True)), axis=1, keepdims=True
    )
    coefficient_limit = CLIP_COEF * norm_scale
    residual_limit = CLIP_RESIDUAL * norm_scale
    factor_inverse = inverse_factor([gram[8 * k : 8 * k + 8] for k in range(16)])
    coeffs = jnp.dot(factor_inverse, cross, preferred_element_type=F32, precision=PRECISE)
    coefficient_squares = jnp.sum(coeffs * coeffs, axis=0, keepdims=True)
    first = lane[:1] < 64
    squares = jnp.concatenate(
        [
            jnp.where(first, pltpu.roll(square[2 * k : 2 * k + 1], 64, 1), square[2 * k + 1 : 2 * k + 2])
            for k in range(4)
        ],
        axis=1,
    )
    residual_squares = jnp.maximum(squares - coefficient_squares, 0.0)
    keep_coefficient = coefficient_limit / jnp.maximum(jnp.sqrt(coefficient_squares), coefficient_limit)
    keep_residual = residual_limit / jnp.maximum(jnp.sqrt(residual_squares), residual_limit)
    weighted = coeffs * (keep_coefficient - keep_residual)
    noise = jnp.where(diagonal, SIGMA_COEF * coefficient_limit * coef_noise[...], 0.0)
    target = jnp.sum(tree([noise] + [weighted[:, 128 * k : 128 * (k + 1)] for k in range(4)]), axis=1, keepdims=True)
    anchor = jnp.sum(target * factor_inverse, axis=0, keepdims=True)
    update = exact_rows(jnp.concatenate([anchor, keep_residual], axis=1), grads_ref[...])
    down = exact_rows(update[:, :256], swap[...])
    gain = 1.0 / math.sqrt(512 * T)
    down_out[...] = (down + SIGMA_RESIDUAL * residual_limit * down_noise[...]) * gain
    up_out[...] = (update[:, 256:] + SIGMA_RESIDUAL * residual_limit * up_noise[...]) * gain


def body(
    public_input_activations,
    public_output_cotangents,
    public_token_lengths,
    private_input_activations,
    private_output_cotangents,
    private_token_lengths,
    adapter_down_matrix,
    adapter_up_matrix,
    embedding_coefficient_noise,
    residual_down_noise,
    residual_up_noise,
):
    dma = pltpu.SemaphoreType.DMA
    v = pltpu.VMEM
    vm = pl.BlockSpec(memory_space=pltpu.VMEM)
    sm = pl.BlockSpec(memory_space=pltpu.SMEM)
    hbm = pl.BlockSpec(memory_space=pltpu.HBM)
    sems = []
    for n in (NX, NY, NS, NS, NY, 1, NY, NZ, NX, NY, 1):
        sems += [dma((n,)), dma((n,))]
    return pl.pallas_call(
        body_kernel,
        out_shape=(jax.ShapeDtypeStruct((1, 256), F32), jax.ShapeDtypeStruct((1, 256), F32)),
        in_specs=[sm, sm] + [hbm] * 6 + [vm] * 3,
        out_specs=(vm, vm),
        scratch_shapes=[
            v((E, T, W), BF), v((E, T, W), BF), v((R, W), BF), v((R, W), BF), dma((12,)),
            v((2, 8, 8, 640), F32), v((640, 512), BF), v((256, 256), BF),
            v((2 * R, 640), F32), v((NX, 2 * R, 640), F32),
            v((NY, 80, 256), BF), v((NY, 80, 256), BF),
            v((NS, 80, 128), BF), v((NS, 80, 128), BF),
            v((NS, 80, 128), BF), v((NS, 80, 128), BF),
            v((NY, 160, 128), BF), v((NY, 160, 128), BF),
            v((2, 8, 8, 640), F32), v((8, 8, 640), F32), v((8, 8, 640), F32), v((NY, 8, 640), F32),
            v((8, 640), F32), v((NZ, 8, 640), F32), v((8, 640), F32), v((NX, 8, 640), F32), v((8, 640), F32),
        ] + sems,
        compiler_params=pltpu.CompilerParams(collective_id=0, has_side_effects=True, vmem_limit_bytes=60 * 1024 * 1024),
    )(
        public_token_lengths, private_token_lengths,
        public_input_activations, public_output_cotangents,
        private_input_activations, private_output_cotangents,
        adapter_down_matrix.T, adapter_up_matrix,
        embedding_coefficient_noise[None], residual_down_noise, residual_up_noise,
    )


def solution(mesh):
    placed = (
        P("dp", None, "mp"),
        P("dp", None, "mp"),
        P("dp"),
        P("dp", None, "mp"),
        P("dp", None, "mp"),
        P("dp"),
        P("mp", None),
        P(None, "mp"),
        P(),
        P("mp", "dp"),
        P("mp", "dp"),
    )
    return jax.shard_map(
        body, mesh=mesh, in_specs=placed, out_specs=(P("mp", "dp"), P("mp", "dp")), check_vma=False
    )
```

```python
import math

import jax
import jax.numpy as jnp
from jax import lax
from jax.experimental import pallas as pl
from jax.experimental.pallas import tpu as pltpu
from jax.sharding import PartitionSpec as P

CLIP_COEF = 0.5
CLIP_RESIDUAL = 0.7
SIGMA_COEF = 1.0
SIGMA_RESIDUAL = 0.04
PRECISE = lax.Precision.HIGHEST
BF, F32 = jnp.bfloat16, jnp.float32
NX, NY, NZ, NC = 4, 8, 8, 2
NS = NZ * NC
E = 5
SPLIT = 5
N_SHARES = 32
T = 112
GROUPS = ((0, 1), (1, 3), (3, 5))
W = 2048
R = 16
MESH = pl.DeviceIdType.MESH


def lane_blocks(rows):
    rows = list(rows)
    block = lax.broadcasted_iota(jnp.int32, rows[0].shape, rows[0].ndim - 1) // R
    axis = rows[0].ndim - 1
    for bit in (1, 2, 4):
        low = (block & bit) == 0
        fresh = list(rows)
        for i in range(8):
            if i & bit:
                continue
            j = i | bit
            fresh[i] = jnp.where(low, rows[i], pltpu.roll(rows[j], R * bit, axis))
            fresh[j] = jnp.where(low, pltpu.roll(rows[i], 128 - R * bit, axis), rows[j])
        rows = fresh
    return rows


def spread_lane(v, j):
    return jnp.broadcast_to(v[:, j : j + 1], v.shape)


def spread_row(v, i):
    return jnp.broadcast_to(v[i : i + 1], v.shape)


def tree(terms):
    terms = list(terms)
    while len(terms) > 1:
        terms = [sum(terms[i + 1 : i + 2], terms[i]) for i in range(0, len(terms), 2)]
    return terms[0]


def stacked(rows, sub):
    for bit in (1, 2, 4):
        odd = (sub & bit) != 0
        rows = [jnp.where(odd, rows[i + 1], rows[i]) for i in range(0, len(rows), 2)]
    return rows[0]


def inverse_factor(g, right, first, last):
    g, right = list(g), list(right)
    shape = (8, 128)
    sub = lax.broadcasted_iota(jnp.int32, shape, 0)
    zero = jnp.zeros(shape, F32)
    out = []
    for k in range(first, last):
        top, edge = g[k], right[k]
        cols = [spread_lane(top, 8 * k + j) for j in range(8)]
        a = {(i, j): spread_row(cols[j], i) for j in range(8) for i in range(j, 8)}
        inv = {}
        low = {}
        for j in range(8):
            p = a[j, j]
            r = lax.rsqrt(p)
            r = r * (1.5 - 0.5 * p * r * r)
            inv[j, j] = r
            for i in range(j + 1, 8):
                low[i, j] = a[i, j] * r
            for m in range(j + 1, 8):
                for i in range(m, 8):
                    a[i, m] = a[i, m] - low[i, j] * low[m, j]
            for i in range(j):
                inv[j, i] = -r * tree([low[j, m] * inv[m, i] for m in range(i, j)])
        top_rows = [spread_row(top, j) for j in range(8)]
        edge_rows = [spread_row(edge, j) for j in range(8)]
        inv_cols = [stacked([inv.get((i, j), zero) for i in range(8)], sub) for j in range(8)]
        edge = tree([inv_cols[j] * edge_rows[j] for j in range(8)])
        out.append(edge)
        if k == 15:
            break
        top = tree([inv_cols[j] * top_rows[j] for j in range(8)])
        top_rows = [spread_row(top, j) for j in range(8)]
        edge_rows = [spread_row(edge, j) for j in range(8)]
        for m in range(k + 1, 16):
            raw = [spread_lane(g[m], 8 * k + j) for j in range(8)]
            factors = [tree([raw[i] * inv[j, i] for i in range(j + 1)]) for j in range(8)]
            g[m] = g[m] - tree([factors[j] * top_rows[j] for j in range(8)])
            right[m] = right[m] - tree([factors[j] * edge_rows[j] for j in range(8)])
    return out, g, right


def split(v):
    high = v.astype(BF)
    rest = v - high.astype(F32)
    middle = rest.astype(BF)
    return high, middle, (rest - middle.astype(F32)).astype(BF)


def exact_rows(row, matrix):
    terms = [t.astype(F32) for t in split(row)]
    terms = jnp.concatenate(terms + [jnp.zeros((5, row.shape[1]), F32)], axis=0).astype(BF)
    out = jnp.dot(terms, matrix, preferred_element_type=F32)
    return out[0:1] + out[1:2] + out[2:3]


def body_kernel(
    pub_len, priv_len, pub_in_hbm, pub_cot_hbm, priv_in_hbm, priv_cot_hbm, down_hbm, up_hbm,
    coef_noise, down_noise, up_noise,
    down_out, up_out,
    ins, cots, down_mat, up_mat, load_sem, grads_ref, swap,
    proj, proj_in, d1s, d1r, u1s, u1r, d2s, d2r, u2s, u2r,
    gm, gmr, g1, gyr, g2, gzr, g3, gxr, g4, gfull,
    cm, cmr, c1, car, cbr, c2, caz, cby, c3, cxr, fa, far, fb, fbr, fin,
    s_sem, r_sem,
):
    loads = [
        pltpu.make_async_copy(src, dst, load_sem.at[k])
        for k, (src, dst) in enumerate(
            [(down_hbm, down_mat), (up_hbm, up_mat), (pub_in_hbm.at[0], ins.at[0]), (pub_cot_hbm.at[0], cots.at[0])]
            + [
                pair
                for e in range(4)
                for pair in ((priv_in_hbm.at[e], ins.at[e + 1]), (priv_cot_hbm.at[e], cots.at[e + 1]))
            ]
        )
    ]
    for load in loads:
        load.start()
    x = lax.axis_index("mp")
    d = lax.axis_index("dp")
    y = d // NS
    s = d % NS
    z = s // NC
    c = s % NC

    def at(yy, ss, xx):
        return (yy * NS + ss, xx)

    xs = [lax.rem(x + k, NX) for k in range(NX)]
    ys = [lax.rem(y + k, NY) for k in range(NY)]
    ss = [lax.rem(s + k, NS) for k in range(NS)]
    zs = [lax.rem(z + k, NZ) for k in range(NZ)]
    to_x = [at(y, s, xs[k]) for k in range(NX)]
    to_y = [at(ys[k], s, x) for k in range(NY)]
    to_s = [at(y, ss[k], x) for k in range(NS)]
    to_z = [at(y, zs[k] * NC + c, x) for k in range(NZ)]
    other = 1 - c
    to_c = at(y, z * NC + other, x)

    barrier = pltpu.get_barrier_semaphore()
    for who in to_x[1:] + to_y[1:] + to_s[1:]:
        pl.semaphore_signal(barrier, inc=1, device_id=who, device_id_type=MESH)

    slots = []
    ends = []

    def remote(src, dst, k, who):
        return pltpu.make_async_remote_copy(
            src_ref=src, dst_ref=dst, send_sem=s_sem.at[k], recv_sem=r_sem.at[k], device_id=who, device_id_type=MESH
        )

    def share(pairs, partners, whole):
        k = len(slots)
        slots.append(k)
        for (src, dst), who in zip(pairs, partners):
            remote(src, dst, k, who).start()
        all_of = remote(whole, whole, k, partners[0])
        ends.append(all_of)
        return all_of.wait_recv

    loads[0].wait()
    loads[1].wait()
    wait_x = []

    def project(e):
        loads[2 + 2 * e].wait()
        loads[3 + 2 * e].wait()
        p = lax.dot_general(ins[e], down_mat[...], (((1,), (1,)), ((), ())), preferred_element_type=F32)
        r = lax.dot_general(cots[e], up_mat[...], (((1,), (1,)), ((), ())), preferred_element_type=F32)
        both = jnp.concatenate([p, r, jnp.zeros((T, 128 - 2 * R), F32)], axis=1)
        both = jnp.concatenate([both, jnp.zeros((128 - T, 128), F32)], axis=0)
        both = both.T[: 2 * R]
        proj[:, 128 * e : 128 * (e + 1)] = both
        proj_in[x, :, 128 * e : 128 * (e + 1)] = both

    def send_x(low, high):
        lanes = slice(128 * low, 128 * high)
        pair = (proj.at[:, lanes], proj_in.at[x, :, lanes])
        wait_x.append(share([pair] * (NX - 1), to_x[1:], proj_in.at[: NX - 1, :, lanes]))

    for e in range(3):
        project(e)
    pl.semaphore_wait(barrier, NX + NY + NS - 3)
    send_x(*GROUPS[0])
    send_x(*GROUPS[1])
    for e in range(3, 5):
        project(e)
    send_x(*GROUPS[2])

    before = lax.broadcasted_iota(jnp.int32, (256, 256), 0)
    after = lax.broadcasted_iota(jnp.int32, (256, 256), 1)
    swap[...] = ((before % R == after // R) & (before // R == after % R)).astype(BF)

    token = lax.broadcasted_iota(jnp.int32, (2 * R, 128), 1)
    row = lax.broadcasted_iota(jnp.int32, (R, R), 0)
    col = lax.broadcasted_iota(jnp.int32, (R, R), 1)
    order = (col == 2 * (row % 8) + row // 8).astype(BF)
    lane = lax.broadcasted_iota(jnp.int32, (8, 128), 1)
    sub = lax.broadcasted_iota(jnp.int32, (8, 128), 0)
    norms = jnp.zeros((8, 128), F32)
    wait_d1, wait_u1, wait_d2, wait_u2 = [], [], [], []
    for (low, high), arrived in zip(GROUPS, wait_x):
        arrived()
        for e in range(low, high):
            lanes = slice(128 * e, 128 * (e + 1))
            total = proj_in[0, :, lanes] + proj_in[1, :, lanes] + proj_in[2, :, lanes] + proj_in[3, :, lanes]
            length = pub_len[0] if e == 0 else priv_len[e - 1]
            live = (total * (token < length).astype(F32)).astype(BF)
            pt = jnp.dot(order, live[:R], preferred_element_type=F32).astype(BF)
            rt = live[R:]
            gd = jnp.dot(rt[:, :T], ins[e], preferred_element_type=F32).astype(BF)
            for k in range(NY):
                d1s[k, R * e : R * (e + 1), :] = gd[:, 256 * k : 256 * (k + 1)]
            gu = jnp.dot(pt[:, :T], cots[e], preferred_element_type=F32).astype(BF).astype(F32)
            for k in range(NS):
                hi, lo = k // 8, k % 8
                rows = gu[8 * hi : 8 * hi + 8]
                pair = jnp.concatenate(
                    [rows[:, 256 * lo : 256 * lo + 128], rows[:, 256 * lo + 128 : 256 * lo + 256]], axis=0
                )
                u1s[k, R * e : R * (e + 1), :] = pair.astype(BF)
            if e:
                wide = gd.astype(F32)
                wide = wide * wide + gu * gu
                wide = tree([wide[:, 128 * k : 128 * (k + 1)] for k in range(16)])
                square = jnp.sum(jnp.sum(wide, axis=0, keepdims=True), axis=1, keepdims=True)
                here = (sub == (e - 1) * 2 + d // 64) & (lane == 64 + d % 64)
                norms = norms + jnp.where(here, square, 0.0)
        rows = slice(R * low, R * high)
        wait_d1.append(
            share(
                [(d1s.at[ys[k], rows], d1r.at[y, rows]) for k in range(1, NY)], to_y[1:], d1r.at[: NY - 1, rows]
            )
        )
        wait_u1.append(
            share(
                [(u1s.at[ss[k], rows], u1r.at[s, rows]) for k in range(1, NS)], to_s[1:], u1r.at[: NS - 1, rows]
            )
        )
        d1r[y, rows] = d1s[y, rows]
        u1r[s, rows] = u1s[s, rows]

    def flip(ref, e, h):
        cube = jnp.stack([ref[k, R * e : R * (e + 1), :].astype(F32)[8 * h : 8 * h + 8] for k in range(NS)], axis=0)
        return jnp.swapaxes(cube, 0, 1).astype(BF)

    for g, (low, high) in enumerate(GROUPS):
        wait_d1[g]()
        for e in range(low, high):
            for hi in range(2):
                tiles = [d1r[k, R * e : R * (e + 1), 128 * hi : 128 * (hi + 1)].astype(F32) for k in range(NY)]
                halves = []
                for rh in range(2):
                    cube = jnp.stack([t[8 * rh : 8 * rh + 8] for t in tiles], axis=0)
                    cube = jnp.swapaxes(cube, 0, 1)
                    halves.append(lane_blocks([cube[i] for i in range(8)]))
                for lo in range(8):
                    pair = jnp.concatenate([halves[0][lo], halves[1][lo]], axis=0)
                    d2s[8 * hi + lo, R * e : R * (e + 1), :] = pair.astype(BF)
        rows = slice(R * low, R * high)
        wait_d2.append(
            share(
                [(d2s.at[ss[k], rows], d2r.at[s, rows]) for k in range(1, NS)], to_s[1:], d2r.at[: NS - 1, rows]
            )
        )
        d2r[s, rows] = d2s[s, rows]
        wait_u1[g]()
        for e in range(low, high):
            for h in range(2):
                k = 2 * e + h
                u2s[:, R * k : R * (k + 1), :] = flip(u1r, e, h)
        rows = slice(2 * R * low, 2 * R * high)
        wait_u2.append(
            share(
                [(u2s.at[ys[k], rows], u2r.at[y, rows]) for k in range(1, NY)], to_y[1:], u2r.at[: NY - 1, rows]
            )
        )
        u2r[y, rows] = u2s[y, rows]

    def assemble(g):
        wait_d2[g]()
        wait_u2[g]()
        for e in range(*GROUPS[g]):
            for h in range(2):
                k = 2 * e + h
                rows = slice(128 * e, 128 * (e + 1))
                grads_ref[rows, 128 * h : 128 * (h + 1)] = flip(d2r, e, h).reshape(128, 128)
                grads_ref[rows, 256 + 128 * h : 256 + 128 * (h + 1)] = u2r[:, R * k : R * (k + 1), :].reshape(128, 128)

    def times_public(rows):
        return lax.dot_general(rows, grads_ref[:128], (((1,), (1,)), ((), ())), preferred_element_type=F32)

    def added(ref):
        n = ref.shape[0]
        return sum([ref[k] for k in range(1, n)], ref[0])

    def spread(src, dst, me, partners):
        dst[me] = src[...]
        return share([(src, dst.at[me])] * len(partners), partners, dst.at[: len(partners)])

    assemble(0)
    gram = times_public(grads_ref[:128])
    gm[...] = gram.reshape(2, 8, 8, 128)
    gm[0, 0] = jnp.where(lane >= 64, norms, gram[:8])
    wait = share([(gm.at[other], gmr)], [to_c], gmr)
    wait()
    g1[...] = gm[c] + gmr[...]
    gyr[y] = g1[y]
    wait = share([(g1.at[ys[k]], gyr.at[y]) for k in range(1, NY)], to_y[1:], gyr.at[: NY - 1])
    assemble(1)
    cm[0] = times_public(grads_ref[128:384]).reshape(2, 8, 16, 128)
    wait()
    g2[...] = added(gyr)
    wait = spread(g2, gzr, z, to_z[1:])
    assemble(2)
    cm[1] = times_public(grads_ref[384:640]).reshape(2, 8, 16, 128)
    wait_c = share([(cm.at[other], cmr)], [to_c], cmr)
    wait()
    g3[...] = added(gzr)
    wait = spread(g3, gxr, x, to_x[1:])
    wait_c()
    c1[...] = cm[c] + cmr[...]
    car[y] = c1[0, y]
    wait_a = share([(c1.at[0, ys[k]], car.at[y]) for k in range(1, NY)], to_y[1:], car.at[: NY - 1])
    cbr[z] = c1[1, z]
    wait_b = share([(c1.at[1, zs[k]], cbr.at[z]) for k in range(1, NZ)], to_z[1:], cbr.at[: NZ - 1])
    wait()
    g4[...] = added(gxr)
    gfull[c, y] = g4[...]
    wait = share([(g4, gfull.at[c, y])] * (NY - 1), to_y[1:], gfull.at[c, : NY - 1])
    wait()
    wait = share([(gfull.at[c], gfull.at[c])], [to_c], gfull.at[c])
    wait()

    square = gfull[...].reshape(128, 128)
    down128 = lax.broadcasted_iota(jnp.int32, (128, 128), 0)
    over128 = lax.broadcasted_iota(jnp.int32, (128, 128), 1)
    gram = jnp.where(over128 > down128, square.T, square)
    diagonal = over128 == down128
    norm_scale = jnp.mean(
        jnp.sqrt(jnp.sum(jnp.where(diagonal, gram, 0.0), axis=0, keepdims=True)), axis=1, keepdims=True
    )
    coefficient_limit = CLIP_COEF * norm_scale
    residual_limit = CLIP_RESIDUAL * norm_scale
    unit = diagonal.astype(F32)
    blocks = [gram[8 * k : 8 * k + 8] for k in range(16)]
    units = [unit[8 * k : 8 * k + 8] for k in range(16)]
    half, blocks, units = inverse_factor(blocks, units, 0, SPLIT)
    wait_a()
    c2[0] = added(car)
    wait_a = spread(c2.at[0], caz, z, to_z[1:])
    wait_b()
    c2[1] = added(cbr)
    wait_b = spread(c2.at[1], cby, y, to_y[1:])
    rest, _, _ = inverse_factor(blocks, units, SPLIT, 16)
    factor_inverse = jnp.concatenate(half + rest, axis=0)
    wait_a()
    c3[0] = added(caz)
    wait_b()
    c3[1] = added(cby)
    wait = spread(c3, cxr, x, to_x[1:])
    wait()
    cross = added(cxr).reshape(32, 128)

    coeffs = lax.dot_general(
        cross, factor_inverse, (((1,), (1,)), ((), ())), preferred_element_type=F32, precision=PRECISE
    )
    coefficient_squares = jnp.sum(coeffs * coeffs, axis=1, keepdims=True)
    lane16 = lax.broadcasted_iota(jnp.int32, (16, 128), 1)
    sub16 = lax.broadcasted_iota(jnp.int32, (16, 128), 0)

    def own_squares(row, place):
        mine = jnp.sum(jnp.where(sub == row, square[:8], 0.0), axis=0, keepdims=True)
        return jnp.sum(jnp.where(lane16 == 64 + place * 16 + sub16, mine, 0.0), axis=1, keepdims=True)

    squares = jnp.concatenate(
        [own_squares(c * 4 + y // 4, y % 4), own_squares(c * 4 + 2 + z // 4, z % 4)], axis=0
    )
    residual_squares = jnp.maximum(squares - coefficient_squares, 0.0)
    keep_coefficient = coefficient_limit / jnp.maximum(jnp.sqrt(coefficient_squares), coefficient_limit)
    keep_residual = residual_limit / jnp.maximum(jnp.sqrt(residual_squares), residual_limit)
    weighted = coeffs * (keep_coefficient - keep_residual)

    def packed(part, place):
        correction = jnp.sum(weighted[part], axis=0, keepdims=True)
        keep = jnp.sum(jnp.where(lane16 == place * 16 + sub16, keep_residual[part], 0.0), axis=0, keepdims=True)
        return jnp.where(sub == 0, correction, jnp.where(sub == 1, keep, 0.0))

    fa[...] = packed(slice(0, 16), y)
    wait_a = spread(fa, far, y, to_y[1:])
    fb[...] = packed(slice(16, 32), z)
    wait_b = spread(fb, fbr, z, to_z[1:])
    wait_a()
    part_a = added(far)
    wait_b()
    part_b = added(fbr)
    fin[c] = jnp.where(sub == 0, part_a + part_b, jnp.where(sub == 1, part_a, pltpu.roll(part_b, 1, 0)))
    wait = share([(fin.at[c], fin.at[c])], [to_c], fin.at[c])
    wait()
    correction = fin[0, 0:1] + fin[1, 0:1]
    target = jnp.sum(
        jnp.where(diagonal, correction + SIGMA_COEF * coefficient_limit * coef_noise[...], 0.0), axis=1, keepdims=True
    )
    anchor = jnp.sum(target * factor_inverse, axis=0, keepdims=True)
    weights = jnp.concatenate([anchor, fin[0, 1:2], fin[0, 2:3], fin[1, 1:2], fin[1, 2:3]], axis=1)
    update = exact_rows(weights, grads_ref[...])
    down = exact_rows(update[:, :256], swap[...])
    gain = 1.0 / math.sqrt(512 * T)
    down_out[...] = (down + SIGMA_RESIDUAL * residual_limit * down_noise[...]) * gain
    up_out[...] = (update[:, 256:] + SIGMA_RESIDUAL * residual_limit * up_noise[...]) * gain
    for copy in ends:
        copy.wait_send()


def body(
    public_input_activations,
    public_output_cotangents,
    public_token_lengths,
    private_input_activations,
    private_output_cotangents,
    private_token_lengths,
    adapter_down_matrix,
    adapter_up_matrix,
    embedding_coefficient_noise,
    residual_down_noise,
    residual_up_noise,
):
    dma = pltpu.SemaphoreType.DMA
    v = pltpu.VMEM
    vm = pl.BlockSpec(memory_space=pltpu.VMEM)
    sm = pl.BlockSpec(memory_space=pltpu.SMEM)
    hbm = pl.BlockSpec(memory_space=pltpu.HBM)
    return pl.pallas_call(
        body_kernel,
        out_shape=(jax.ShapeDtypeStruct((1, 256), F32), jax.ShapeDtypeStruct((1, 256), F32)),
        in_specs=[sm, sm] + [hbm] * 6 + [vm] * 3,
        out_specs=(vm, vm),
        scratch_shapes=[
            v((E, T, W), BF), v((E, T, W), BF), v((R, W), BF), v((R, W), BF), dma((12,)),
            v((640, 512), BF), v((256, 256), BF),
            v((2 * R, 640), F32), v((NX, 2 * R, 640), F32),
            v((NY, 80, 256), BF), v((NY, 80, 256), BF),
            v((NS, 80, 128), BF), v((NS, 80, 128), BF),
            v((NS, 80, 128), BF), v((NS, 80, 128), BF),
            v((NY, 160, 128), BF), v((NY, 160, 128), BF),
            v((2, 8, 8, 128), F32), v((8, 8, 128), F32), v((8, 8, 128), F32), v((NY, 8, 128), F32),
            v((8, 128), F32), v((NZ, 8, 128), F32), v((8, 128), F32), v((NX, 8, 128), F32), v((8, 128), F32),
            v((2, 8, 8, 128), F32),
            v((2, 2, 8, 16, 128), F32), v((2, 8, 16, 128), F32), v((2, 8, 16, 128), F32),
            v((NY, 16, 128), F32), v((NZ, 16, 128), F32), v((2, 16, 128), F32),
            v((NZ, 16, 128), F32), v((NY, 16, 128), F32), v((2, 16, 128), F32), v((NX, 2, 16, 128), F32),
            v((8, 128), F32), v((NY, 8, 128), F32), v((8, 128), F32), v((NZ, 8, 128), F32), v((2, 8, 128), F32),
            dma((N_SHARES,)), dma((N_SHARES,)),
        ],
        compiler_params=pltpu.CompilerParams(collective_id=0, has_side_effects=True, vmem_limit_bytes=60 * 1024 * 1024),
    )(
        public_token_lengths, private_token_lengths,
        public_input_activations, public_output_cotangents,
        private_input_activations, private_output_cotangents,
        adapter_down_matrix.T, adapter_up_matrix,
        embedding_coefficient_noise[None], residual_down_noise, residual_up_noise,
    )


def solution(mesh):
    placed = (
        P("dp", None, "mp"),
        P("dp", None, "mp"),
        P("dp"),
        P("dp", None, "mp"),
        P("dp", None, "mp"),
        P("dp"),
        P("mp", None),
        P(None, "mp"),
        P(),
        P("mp", "dp"),
        P("mp", "dp"),
    )
    return jax.shard_map(
        body, mesh=mesh, in_specs=placed, out_specs=(P("mp", "dp"), P("mp", "dp")), check_vma=False
    )
```

```python
import math

import jax
import jax.numpy as jnp
from jax import lax
from jax.experimental import pallas as pl
from jax.experimental.pallas import tpu as pltpu
from jax.sharding import PartitionSpec as P

CLIP_COEF = 0.5
CLIP_RESIDUAL = 0.7
SIGMA_COEF = 1.0
SIGMA_RESIDUAL = 0.04
PRECISE = lax.Precision.HIGHEST
BF, F32 = jnp.bfloat16, jnp.float32
NX, NY, NZ, NC = 4, 8, 8, 2
NS = NZ * NC
E = 5
N_SHARES = 32
T = 112
GROUPS = ((0, 1), (1, 3), (3, 5))
W = 2048
R = 16
MESH = pl.DeviceIdType.MESH


def lane_blocks(rows):
    rows = list(rows)
    block = lax.broadcasted_iota(jnp.int32, rows[0].shape, rows[0].ndim - 1) // R
    axis = rows[0].ndim - 1
    for bit in (1, 2, 4):
        low = (block & bit) == 0
        fresh = list(rows)
        for i in range(8):
            if i & bit:
                continue
            j = i | bit
            fresh[i] = jnp.where(low, rows[i], pltpu.roll(rows[j], R * bit, axis))
            fresh[j] = jnp.where(low, pltpu.roll(rows[i], 128 - R * bit, axis), rows[j])
        rows = fresh
    return rows


def spread_lane(v, j):
    return jnp.broadcast_to(v[:, j : j + 1], v.shape)


def spread_row(v, i):
    return jnp.broadcast_to(v[i : i + 1], v.shape)


def tree(terms):
    terms = list(terms)
    while len(terms) > 1:
        terms = [sum(terms[i + 1 : i + 2], terms[i]) for i in range(0, len(terms), 2)]
    return terms[0]


def stacked(rows, sub):
    for bit in (1, 2, 4):
        odd = (sub & bit) != 0
        rows = [jnp.where(odd, rows[i + 1], rows[i]) for i in range(0, len(rows), 2)]
    return rows[0]


def inverse_factor(g, right):
    g, right = list(g), list(right)
    shape = (8, 128)
    sub = lax.broadcasted_iota(jnp.int32, shape, 0)
    zero = jnp.zeros(shape, F32)
    out = []
    for k in range(16):
        top, edge = g[k], right[k]
        cols = [spread_lane(top, 8 * k + j) for j in range(8)]
        a = {(i, j): spread_row(cols[j], i) for j in range(8) for i in range(j, 8)}
        inv = {}
        low = {}
        for j in range(8):
            p = a[j, j]
            r = lax.rsqrt(p)
            r = r * (1.5 - 0.5 * p * r * r)
            inv[j, j] = r
            for i in range(j + 1, 8):
                low[i, j] = a[i, j] * r
            for m in range(j + 1, 8):
                for i in range(m, 8):
                    a[i, m] = a[i, m] - low[i, j] * low[m, j]
            for i in range(j):
                inv[j, i] = -r * tree([low[j, m] * inv[m, i] for m in range(i, j)])
        top_rows = [spread_row(top, j) for j in range(8)]
        edge_rows = [spread_row(edge, j) for j in range(8)]
        inv_cols = [stacked([inv.get((i, j), zero) for i in range(8)], sub) for j in range(8)]
        edge = tree([inv_cols[j] * edge_rows[j] for j in range(8)])
        out.append(edge)
        if k == 15:
            break
        top = tree([inv_cols[j] * top_rows[j] for j in range(8)])
        top_rows = [spread_row(top, j) for j in range(8)]
        edge_rows = [spread_row(edge, j) for j in range(8)]
        for m in range(k + 1, 16):
            raw = [spread_lane(g[m], 8 * k + j) for j in range(8)]
            factors = [tree([raw[i] * inv[j, i] for i in range(j + 1)]) for j in range(8)]
            g[m] = g[m] - tree([factors[j] * top_rows[j] for j in range(8)])
            right[m] = right[m] - tree([factors[j] * edge_rows[j] for j in range(8)])
    return out


def split(v):
    high = v.astype(BF)
    rest = v - high.astype(F32)
    middle = rest.astype(BF)
    return high, middle, (rest - middle.astype(F32)).astype(BF)


def exact_rows(row, matrix):
    terms = [t.astype(F32) for t in split(row)]
    terms = jnp.concatenate(terms + [jnp.zeros((5, row.shape[1]), F32)], axis=0).astype(BF)
    out = jnp.dot(terms, matrix, preferred_element_type=F32)
    return out[0:1] + out[1:2] + out[2:3]


def body_kernel(
    pub_len_hbm, priv_len_hbm, pub_in_hbm, pub_cot_hbm, priv_in_hbm, priv_cot_hbm, down_hbm, up_hbm,
    coef_hbm, down_noise_hbm, up_noise_hbm,
    out,
    pub_len, priv_len, coef_noise, down_noise, up_noise,
    ins, cots, down_mat, up_mat, load_sem, small_sem, grads_ref, swap,
    proj, proj_in, d1s, d1r, u1s, u1r, d2s, d2r, u2s, u2r,
    gm, gyr, g2, gzr, g3, gxr, g4, gfull,
    cm, cmr, c1, car, cbr, c2, caz, cby, c3, cxr, fa, far, fb, fbr,
    s_sem, r_sem,
):
    loads = [
        pltpu.make_async_copy(src, dst, load_sem.at[k])
        for k, (src, dst) in enumerate(
            [(down_hbm, down_mat), (up_hbm, up_mat), (pub_in_hbm.at[0], ins.at[0]), (pub_cot_hbm.at[0], cots.at[0])]
            + [
                pair
                for e in range(4)
                for pair in ((priv_in_hbm.at[e], ins.at[e + 1]), (priv_cot_hbm.at[e], cots.at[e + 1]))
            ]
        )
    ]
    small = [
        pltpu.make_async_copy(src, dst, small_sem.at[k])
        for k, (src, dst) in enumerate(
            [
                (pub_len_hbm, pub_len), (priv_len_hbm, priv_len),
                (coef_hbm, coef_noise), (down_noise_hbm, down_noise), (up_noise_hbm, up_noise),
            ]
        )
    ]
    for load in loads + small:
        load.start()
    x = lax.axis_index("mp")
    d = lax.axis_index("dp")
    y = d // NS
    s = d % NS
    z = s // NC
    c = s % NC

    def at(yy, ss, xx):
        return (yy * NS + ss, xx)

    xs = [lax.rem(x + k, NX) for k in range(NX)]
    ys = [lax.rem(y + k, NY) for k in range(NY)]
    ss = [lax.rem(s + k, NS) for k in range(NS)]
    zs = [lax.rem(z + k, NZ) for k in range(NZ)]
    to_x = [at(y, s, xs[k]) for k in range(NX)]
    to_y = [at(ys[k], s, x) for k in range(NY)]
    to_s = [at(y, ss[k], x) for k in range(NS)]
    to_z = [at(y, zs[k] * NC + c, x) for k in range(NZ)]
    other = 1 - c
    to_c = at(y, z * NC + other, x)
    q = y * NC + c
    turns = [(ky, kc) for ky in range(NY) for kc in range(NC)][1:]
    qs = [ys[ky] * NC + lax.rem(c + kc, NC) for ky, kc in turns]
    to_q = [at(ys[ky], z * NC + lax.rem(c + kc, NC), x) for ky, kc in turns]

    barrier = pltpu.get_barrier_semaphore()
    greeted = to_x[1:] + to_q[1:] + to_s[1:]
    for who in greeted:
        pl.semaphore_signal(barrier, inc=1, device_id=who, device_id_type=MESH)

    slots = []
    ends = []

    def remote(src, dst, k, who):
        return pltpu.make_async_remote_copy(
            src_ref=src, dst_ref=dst, send_sem=s_sem.at[k], recv_sem=r_sem.at[k], device_id=who, device_id_type=MESH
        )

    def share(pairs, partners, whole):
        k = len(slots)
        slots.append(k)
        for (src, dst), who in zip(pairs, partners):
            remote(src, dst, k, who).start()
        all_of = remote(whole, whole, k, partners[0])
        ends.append(all_of)
        return all_of.wait_recv

    loads[0].wait()
    loads[1].wait()
    wait_x = []

    def project(e):
        loads[2 + 2 * e].wait()
        loads[3 + 2 * e].wait()
        p = lax.dot_general(ins[e], down_mat[...], (((1,), (1,)), ((), ())), preferred_element_type=F32)
        r = lax.dot_general(cots[e], up_mat[...], (((1,), (1,)), ((), ())), preferred_element_type=F32)
        both = jnp.concatenate([p, r, jnp.zeros((T, 128 - 2 * R), F32)], axis=1)
        both = jnp.concatenate([both, jnp.zeros((128 - T, 128), F32)], axis=0)
        both = both.T[: 2 * R]
        proj[:, 128 * e : 128 * (e + 1)] = both
        proj_in[x, :, 128 * e : 128 * (e + 1)] = both

    def send_x(low, high):
        lanes = slice(128 * low, 128 * high)
        pair = (proj.at[:, lanes], proj_in.at[x, :, lanes])
        wait_x.append(share([pair] * (NX - 1), to_x[1:], proj_in.at[: NX - 1, :, lanes]))

    for e in range(3):
        project(e)
    pl.semaphore_wait(barrier, len(greeted))
    send_x(*GROUPS[0])
    send_x(*GROUPS[1])
    for e in range(3, 5):
        project(e)
    send_x(*GROUPS[2])

    for load in small:
        load.wait()
    before = lax.broadcasted_iota(jnp.int32, (256, 256), 0)
    after = lax.broadcasted_iota(jnp.int32, (256, 256), 1)
    swap[...] = ((before % R == after // R) & (before // R == after % R)).astype(BF)

    token = lax.broadcasted_iota(jnp.int32, (2 * R, 128), 1)
    row = lax.broadcasted_iota(jnp.int32, (R, R), 0)
    col = lax.broadcasted_iota(jnp.int32, (R, R), 1)
    order = (col == 2 * (row % 8) + row // 8).astype(BF)
    lane = lax.broadcasted_iota(jnp.int32, (8, 128), 1)
    sub = lax.broadcasted_iota(jnp.int32, (8, 128), 0)
    norms = jnp.zeros((8, 128), F32)
    wait_d1, wait_u1, wait_d2, wait_u2 = [], [], [], []
    for (low, high), arrived in zip(GROUPS, wait_x):
        arrived()
        for e in range(low, high):
            lanes = slice(128 * e, 128 * (e + 1))
            total = proj_in[0, :, lanes] + proj_in[1, :, lanes] + proj_in[2, :, lanes] + proj_in[3, :, lanes]
            length = pub_len[0] if e == 0 else priv_len[e - 1]
            live = (total * (token < length).astype(F32)).astype(BF)
            pt = jnp.dot(order, live[:R], preferred_element_type=F32).astype(BF)
            rt = live[R:]
            gd = jnp.dot(rt[:, :T], ins[e], preferred_element_type=F32).astype(BF)
            for k in range(NY):
                d1s[k, R * e : R * (e + 1), :] = gd[:, 256 * k : 256 * (k + 1)]
            gu = jnp.dot(pt[:, :T], cots[e], preferred_element_type=F32).astype(BF).astype(F32)
            for k in range(NS):
                hi, lo = k // 8, k % 8
                rows = gu[8 * hi : 8 * hi + 8]
                pair = jnp.concatenate(
                    [rows[:, 256 * lo : 256 * lo + 128], rows[:, 256 * lo + 128 : 256 * lo + 256]], axis=0
                )
                u1s[k, R * e : R * (e + 1), :] = pair.astype(BF)
            if e:
                wide = gd.astype(F32)
                wide = wide * wide + gu * gu
                wide = tree([wide[:, 128 * k : 128 * (k + 1)] for k in range(16)])
                square = jnp.sum(jnp.sum(wide, axis=0, keepdims=True), axis=1, keepdims=True)
                here = (sub == (e - 1) * 2 + d // 64) & (lane == 64 + d % 64)
                norms = norms + jnp.where(here, square, 0.0)
        rows = slice(R * low, R * high)
        wait_d1.append(
            share(
                [(d1s.at[ys[k], rows], d1r.at[y, rows]) for k in range(1, NY)], to_y[1:], d1r.at[: NY - 1, rows]
            )
        )
        wait_u1.append(
            share(
                [(u1s.at[ss[k], rows], u1r.at[s, rows]) for k in range(1, NS)], to_s[1:], u1r.at[: NS - 1, rows]
            )
        )
        d1r[y, rows] = d1s[y, rows]
        u1r[s, rows] = u1s[s, rows]

    def flip(ref, e, h):
        cube = jnp.stack([ref[k, R * e : R * (e + 1), :].astype(F32)[8 * h : 8 * h + 8] for k in range(NS)], axis=0)
        return jnp.swapaxes(cube, 0, 1).astype(BF)

    for g, (low, high) in enumerate(GROUPS):
        wait_d1[g]()
        for e in range(low, high):
            for hi in range(2):
                tiles = [d1r[k, R * e : R * (e + 1), 128 * hi : 128 * (hi + 1)].astype(F32) for k in range(NY)]
                halves = []
                for rh in range(2):
                    cube = jnp.stack([t[8 * rh : 8 * rh + 8] for t in tiles], axis=0)
                    cube = jnp.swapaxes(cube, 0, 1)
                    halves.append(lane_blocks([cube[i] for i in range(8)]))
                for lo in range(8):
                    pair = jnp.concatenate([halves[0][lo], halves[1][lo]], axis=0)
                    d2s[8 * hi + lo, R * e : R * (e + 1), :] = pair.astype(BF)
        rows = slice(R * low, R * high)
        wait_d2.append(
            share(
                [(d2s.at[ss[k], rows], d2r.at[s, rows]) for k in range(1, NS)], to_s[1:], d2r.at[: NS - 1, rows]
            )
        )
        d2r[s, rows] = d2s[s, rows]
        wait_u1[g]()
        for e in range(low, high):
            for h in range(2):
                k = 2 * e + h
                u2s[:, R * k : R * (k + 1), :] = flip(u1r, e, h)
        rows = slice(2 * R * low, 2 * R * high)
        wait_u2.append(
            share(
                [(u2s.at[ys[k], rows], u2r.at[y, rows]) for k in range(1, NY)], to_y[1:], u2r.at[: NY - 1, rows]
            )
        )
        u2r[y, rows] = u2s[y, rows]

    def assemble(g):
        wait_d2[g]()
        wait_u2[g]()
        for e in range(*GROUPS[g]):
            for h in range(2):
                k = 2 * e + h
                rows = slice(128 * e, 128 * (e + 1))
                grads_ref[rows, 128 * h : 128 * (h + 1)] = flip(d2r, e, h).reshape(128, 128)
                grads_ref[rows, 256 + 128 * h : 256 + 128 * (h + 1)] = u2r[:, R * k : R * (k + 1), :].reshape(128, 128)

    def times_public(rows):
        return lax.dot_general(rows, grads_ref[:128], (((1,), (1,)), ((), ())), preferred_element_type=F32)

    def added(ref):
        n = ref.shape[0]
        return sum([ref[k] for k in range(1, n)], ref[0])

    def spread(src, dst, me, partners):
        dst[me] = src[...]
        return share([(src, dst.at[me])] * len(partners), partners, dst.at[: len(partners)])

    assemble(0)
    gram = times_public(grads_ref[:128])
    gm[...] = gram.reshape(16, 8, 128)
    gm[0] = jnp.where(lane >= 64, norms, gram[:8])
    gyr[q] = gm[q]
    wait = share([(gm.at[to], gyr.at[q]) for to in qs], to_q, gyr.at[: NS - 1])
    assemble(1)
    cm[0] = times_public(grads_ref[128:384]).reshape(2, 8, 16, 128)
    wait()
    g2[...] = added(gyr)
    wait = spread(g2, gzr, z, to_z[1:])
    assemble(2)
    cm[1] = times_public(grads_ref[384:640]).reshape(2, 8, 16, 128)
    wait_c = share([(cm.at[other], cmr)], [to_c], cmr)
    wait()
    g3[...] = added(gzr)
    wait = spread(g3, gxr, x, to_x[1:])
    wait_c()
    c1[...] = cm[c] + cmr[...]
    car[y] = c1[0, y]
    wait_a = share([(c1.at[0, ys[k]], car.at[y]) for k in range(1, NY)], to_y[1:], car.at[: NY - 1])
    cbr[z] = c1[1, z]
    wait_b = share([(c1.at[1, zs[k]], cbr.at[z]) for k in range(1, NZ)], to_z[1:], cbr.at[: NZ - 1])
    wait()
    g4[...] = added(gxr)
    wait = spread(g4, gfull, q, to_q)
    wait_a()
    c2[0] = added(car)
    wait_a = spread(c2.at[0], caz, z, to_z[1:])
    wait_b()
    c2[1] = added(cbr)
    wait_b = spread(c2.at[1], cby, y, to_y[1:])
    wait()

    square = gfull[...].reshape(128, 128)
    down128 = lax.broadcasted_iota(jnp.int32, (128, 128), 0)
    over128 = lax.broadcasted_iota(jnp.int32, (128, 128), 1)
    gram = jnp.where(over128 > down128, square.T, square)
    diagonal = over128 == down128
    norm_scale = jnp.mean(
        jnp.sqrt(jnp.sum(jnp.where(diagonal, gram, 0.0), axis=0, keepdims=True)), axis=1, keepdims=True
    )
    coefficient_limit = CLIP_COEF * norm_scale
    residual_limit = CLIP_RESIDUAL * norm_scale
    unit = diagonal.astype(F32)
    factor_inverse = jnp.concatenate(
        inverse_factor([gram[8 * k : 8 * k + 8] for k in range(16)], [unit[8 * k : 8 * k + 8] for k in range(16)]), axis=0
    )
    wait_a()
    c3[0] = added(caz)
    wait_b()
    c3[1] = added(cby)
    wait = spread(c3, cxr, x, to_x[1:])
    wait()
    cross = added(cxr).reshape(32, 128)

    coeffs = lax.dot_general(
        cross, factor_inverse, (((1,), (1,)), ((), ())), preferred_element_type=F32, precision=PRECISE
    )
    coefficient_squares = jnp.sum(coeffs * coeffs, axis=1, keepdims=True)
    lane16 = lax.broadcasted_iota(jnp.int32, (16, 128), 1)
    sub16 = lax.broadcasted_iota(jnp.int32, (16, 128), 0)

    def own_squares(row, place):
        mine = jnp.sum(jnp.where(sub == row, square[:8], 0.0), axis=0, keepdims=True)
        return jnp.sum(jnp.where(lane16 == 64 + place * 16 + sub16, mine, 0.0), axis=1, keepdims=True)

    squares = jnp.concatenate(
        [own_squares(c * 4 + y // 4, y % 4), own_squares(c * 4 + 2 + z // 4, z % 4)], axis=0
    )
    residual_squares = jnp.maximum(squares - coefficient_squares, 0.0)
    keep_coefficient = coefficient_limit / jnp.maximum(jnp.sqrt(coefficient_squares), coefficient_limit)
    keep_residual = residual_limit / jnp.maximum(jnp.sqrt(residual_squares), residual_limit)
    weighted = coeffs * (keep_coefficient - keep_residual)

    def packed(part, place, row):
        correction = jnp.sum(weighted[part], axis=0, keepdims=True)
        keep = jnp.sum(jnp.where(lane16 == place * 16 + sub16, keep_residual[part], 0.0), axis=0, keepdims=True)
        return jnp.where(sub == 0, correction, jnp.where(sub == row, keep, 0.0))

    fa[...] = packed(slice(0, 16), y, 1 + 2 * c)
    wait_a = spread(fa, far, q, to_q)
    fb[...] = packed(slice(16, 32), z, 2 + 2 * c)
    wait_b = spread(fb, fbr, s, to_s[1:])
    wait_a()
    final = added(far)
    wait_b()
    final = final + added(fbr)
    target = jnp.sum(
        jnp.where(diagonal, final[0:1] + SIGMA_COEF * coefficient_limit * coef_noise[...], 0.0), axis=1, keepdims=True
    )
    anchor = jnp.sum(target * factor_inverse, axis=0, keepdims=True)
    weights = jnp.concatenate([anchor] + [final[k : k + 1] for k in range(1, E)], axis=1)
    update = exact_rows(weights, grads_ref[...])
    down = exact_rows(update[:, :256], swap[...])
    gain = 1.0 / math.sqrt(512 * T)
    out[0:1] = (down + SIGMA_RESIDUAL * residual_limit * down_noise[...]) * gain
    out[1:2] = (update[:, 256:] + SIGMA_RESIDUAL * residual_limit * up_noise[...]) * gain
    for copy in ends:
        copy.wait_send()


def parted_kernel(both, down_out, up_out):
    down_out[...] = both[0:1]
    up_out[...] = both[1:2]


def body(
    public_input_activations,
    public_output_cotangents,
    public_token_lengths,
    private_input_activations,
    private_output_cotangents,
    private_token_lengths,
    adapter_down_matrix,
    adapter_up_matrix,
    embedding_coefficient_noise,
    residual_down_noise,
    residual_up_noise,
):
    dma = pltpu.SemaphoreType.DMA
    v = pltpu.VMEM
    vm = pl.BlockSpec(memory_space=pltpu.VMEM)
    hbm = pl.BlockSpec(memory_space=pltpu.HBM)
    both = pl.pallas_call(
        body_kernel,
        out_shape=jax.ShapeDtypeStruct((2, 256), F32),
        in_specs=[hbm] * 11,
        out_specs=vm,
        scratch_shapes=[
            pltpu.SMEM((1,), jnp.int32), pltpu.SMEM((4,), jnp.int32), v((1, 128), F32), v((1, 256), F32), v((1, 256), F32),
            v((E, T, W), BF), v((E, T, W), BF), v((R, W), BF), v((R, W), BF), dma((12,)), dma((5,)),
            v((640, 512), BF), v((256, 256), BF),
            v((2 * R, 640), F32), v((NX, 2 * R, 640), F32),
            v((NY, 80, 256), BF), v((NY, 80, 256), BF),
            v((NS, 80, 128), BF), v((NS, 80, 128), BF),
            v((NS, 80, 128), BF), v((NS, 80, 128), BF),
            v((NY, 160, 128), BF), v((NY, 160, 128), BF),
            v((16, 8, 128), F32), v((NS, 8, 128), F32),
            v((8, 128), F32), v((NZ, 8, 128), F32), v((8, 128), F32), v((NX, 8, 128), F32), v((8, 128), F32),
            v((16, 8, 128), F32),
            v((2, 2, 8, 16, 128), F32), v((2, 8, 16, 128), F32), v((2, 8, 16, 128), F32),
            v((NY, 16, 128), F32), v((NZ, 16, 128), F32), v((2, 16, 128), F32),
            v((NZ, 16, 128), F32), v((NY, 16, 128), F32), v((2, 16, 128), F32), v((NX, 2, 16, 128), F32),
            v((8, 128), F32), v((NS, 8, 128), F32), v((8, 128), F32), v((NS, 8, 128), F32),
            dma((N_SHARES,)), dma((N_SHARES,)),
        ],
        compiler_params=pltpu.CompilerParams(collective_id=0, has_side_effects=True, vmem_limit_bytes=60 * 1024 * 1024),
    )(
        public_token_lengths, private_token_lengths,
        public_input_activations, public_output_cotangents,
        private_input_activations, private_output_cotangents,
        adapter_down_matrix.T, adapter_up_matrix,
        embedding_coefficient_noise[None], residual_down_noise, residual_up_noise,
    )
    return pl.pallas_call(
        parted_kernel,
        out_shape=(jax.ShapeDtypeStruct((1, 256), F32), jax.ShapeDtypeStruct((1, 256), F32)),
        in_specs=[vm],
        out_specs=(vm, vm),
    )(both)


def solution(mesh):
    placed = (
        P("dp", None, "mp"),
        P("dp", None, "mp"),
        P("dp"),
        P("dp", None, "mp"),
        P("dp", None, "mp"),
        P("dp"),
        P("mp", None),
        P(None, "mp"),
        P(),
        P("mp", "dp"),
        P("mp", "dp"),
    )
    return jax.shard_map(
        body, mesh=mesh, in_specs=placed, out_specs=(P("mp", "dp"), P("mp", "dp")), check_vma=False
    )
```

```python
import math

import jax
import jax.numpy as jnp
from jax import lax
from jax.experimental import pallas as pl
from jax.experimental.pallas import tpu as pltpu
from jax.sharding import PartitionSpec as P

CLIP_COEF = 0.5
CLIP_RESIDUAL = 0.7
SIGMA_COEF = 1.0
SIGMA_RESIDUAL = 0.04
PRECISE = lax.Precision.HIGHEST
BF, F32 = jnp.bfloat16, jnp.float32
NX, NY, NZ, NC = 4, 8, 8, 2
NS = NZ * NC
E = 5
SPLIT = 3
N_SHARES = 32
T = 112
GROUPS = ((0, 1), (1, 3), (3, 5))
W = 2048
R = 16
MESH = pl.DeviceIdType.MESH


def lane_blocks(rows):
    rows = list(rows)
    block = lax.broadcasted_iota(jnp.int32, rows[0].shape, rows[0].ndim - 1) // R
    axis = rows[0].ndim - 1
    for bit in (1, 2, 4):
        low = (block & bit) == 0
        fresh = list(rows)
        for i in range(8):
            if i & bit:
                continue
            j = i | bit
            fresh[i] = jnp.where(low, rows[i], pltpu.roll(rows[j], R * bit, axis))
            fresh[j] = jnp.where(low, pltpu.roll(rows[i], 128 - R * bit, axis), rows[j])
        rows = fresh
    return rows


def spread_lane(v, j):
    return jnp.broadcast_to(v[:, j : j + 1], v.shape)


def spread_row(v, i):
    return jnp.broadcast_to(v[i : i + 1], v.shape)


def tree(terms):
    terms = list(terms)
    while len(terms) > 1:
        terms = [sum(terms[i + 1 : i + 2], terms[i]) for i in range(0, len(terms), 2)]
    return terms[0]


def stacked(rows, sub):
    for bit in (1, 2, 4):
        odd = (sub & bit) != 0
        rows = [jnp.where(odd, rows[i + 1], rows[i]) for i in range(0, len(rows), 2)]
    return rows[0]


def inverse_factor(g, right, first, last):
    g, right = list(g), list(right)
    shape = (8, 128)
    sub = lax.broadcasted_iota(jnp.int32, shape, 0)
    zero = jnp.zeros(shape, F32)
    out = []
    for k in range(first, last):
        top, edge = g[k], right[k]
        cols = [spread_lane(top, 8 * k + j) for j in range(8)]
        a = {(i, j): spread_row(cols[j], i) for j in range(8) for i in range(j, 8)}
        inv = {}
        low = {}
        for j in range(8):
            p = a[j, j]
            r = lax.rsqrt(p)
            r = r * (1.5 - 0.5 * p * r * r)
            inv[j, j] = r
            for i in range(j + 1, 8):
                low[i, j] = a[i, j] * r
            for m in range(j + 1, 8):
                for i in range(m, 8):
                    a[i, m] = a[i, m] - low[i, j] * low[m, j]
            for i in range(j):
                inv[j, i] = -r * tree([low[j, m] * inv[m, i] for m in range(i, j)])
        top_rows = [spread_row(top, j) for j in range(8)]
        edge_rows = [spread_row(edge, j) for j in range(8)]
        inv_cols = [stacked([inv.get((i, j), zero) for i in range(8)], sub) for j in range(8)]
        edge = tree([inv_cols[j] * edge_rows[j] for j in range(8)])
        out.append(edge)
        if k == 15:
            break
        top = tree([inv_cols[j] * top_rows[j] for j in range(8)])
        top_rows = [spread_row(top, j) for j in range(8)]
        edge_rows = [spread_row(edge, j) for j in range(8)]
        turned = [stacked([inv.get((j, i), zero) for i in range(8)], sub) for j in range(8)]
        top = tree([turned[j] * top_rows[j] for j in range(8)])
        edge = tree([turned[j] * edge_rows[j] for j in range(8)])
        top_rows = [spread_row(top, j) for j in range(8)]
        edge_rows = [spread_row(edge, j) for j in range(8)]
        for m in range(k + 1, 16):
            factors = [spread_lane(g[m], 8 * k + j) for j in range(8)]
            g[m] = g[m] - tree([factors[j] * top_rows[j] for j in range(8)])
            right[m] = right[m] - tree([factors[j] * edge_rows[j] for j in range(8)])
    return out, g, right


def split(v):
    high = v.astype(BF)
    rest = v - high.astype(F32)
    middle = rest.astype(BF)
    return high, middle, (rest - middle.astype(F32)).astype(BF)


def exact_rows(row, matrix):
    terms = [t.astype(F32) for t in split(row)]
    terms = jnp.concatenate(terms + [jnp.zeros((5, row.shape[1]), F32)], axis=0).astype(BF)
    out = jnp.dot(terms, matrix, preferred_element_type=F32)
    return out[0:1] + out[1:2] + out[2:3]


def body_kernel(
    pub_len_hbm, priv_len_hbm, pub_in_hbm, pub_cot_hbm, priv_in_hbm, priv_cot_hbm, down_hbm, up_hbm,
    coef_hbm, down_noise_hbm, up_noise_hbm,
    out,
    pub_len, priv_len, coef_noise, down_noise, up_noise,
    ins, cots, down_mat, up_mat, load_sem, small_sem, grads_ref, swap,
    proj, proj_in, d1s, d1r, u1s, u1r, d2s, d2r, u2s, u2r,
    gm, gyr, g2, gzr, g3, gxr, g4, gfull,
    cm, cmr, c1, car, cbr, c2, caz, cby, c3, cxr, fa, far, fb, fbr,
    s_sem, r_sem,
):
    loads = [
        pltpu.make_async_copy(src, dst, load_sem.at[k])
        for k, (src, dst) in enumerate(
            [(down_hbm, down_mat), (up_hbm, up_mat), (pub_in_hbm.at[0], ins.at[0]), (pub_cot_hbm.at[0], cots.at[0])]
            + [
                pair
                for e in range(4)
                for pair in ((priv_in_hbm.at[e], ins.at[e + 1]), (priv_cot_hbm.at[e], cots.at[e + 1]))
            ]
        )
    ]
    small = [
        pltpu.make_async_copy(src, dst, small_sem.at[k])
        for k, (src, dst) in enumerate(
            [
                (pub_len_hbm, pub_len), (priv_len_hbm, priv_len),
                (coef_hbm, coef_noise), (down_noise_hbm, down_noise), (up_noise_hbm, up_noise),
            ]
        )
    ]
    for load in loads + small:
        load.start()
    x = lax.axis_index("mp")
    d = lax.axis_index("dp")
    y = d // NS
    s = d % NS
    z = s // NC
    c = s % NC

    def at(yy, ss, xx):
        return (yy * NS + ss, xx)

    xs = [lax.rem(x + k, NX) for k in range(NX)]
    ys = [lax.rem(y + k, NY) for k in range(NY)]
    ss = [lax.rem(s + k, NS) for k in range(NS)]
    zs = [lax.rem(z + k, NZ) for k in range(NZ)]
    to_x = [at(y, s, xs[k]) for k in range(NX)]
    to_y = [at(ys[k], s, x) for k in range(NY)]
    to_s = [at(y, ss[k], x) for k in range(NS)]
    to_z = [at(y, zs[k] * NC + c, x) for k in range(NZ)]
    other = 1 - c
    to_c = at(y, z * NC + other, x)
    q = y * NC + c
    turns = [(ky, kc) for ky in range(NY) for kc in range(NC)][1:]
    qs = [ys[ky] * NC + lax.rem(c + kc, NC) for ky, kc in turns]
    to_q = [at(ys[ky], z * NC + lax.rem(c + kc, NC), x) for ky, kc in turns]

    barrier = pltpu.get_barrier_semaphore()
    greeted = to_x[1:] + to_q[1:] + to_s[1:]
    for who in greeted:
        pl.semaphore_signal(barrier, inc=1, device_id=who, device_id_type=MESH)

    slots = []
    ends = []

    def remote(src, dst, k, who):
        return pltpu.make_async_remote_copy(
            src_ref=src, dst_ref=dst, send_sem=s_sem.at[k], recv_sem=r_sem.at[k], device_id=who, device_id_type=MESH
        )

    def share(pairs, partners, whole):
        k = len(slots)
        slots.append(k)
        for (src, dst), who in zip(pairs, partners):
            remote(src, dst, k, who).start()
        all_of = remote(whole, whole, k, partners[0])
        ends.append(all_of)
        return all_of.wait_recv

    loads[0].wait()
    loads[1].wait()
    wait_x = []

    def project(e):
        loads[2 + 2 * e].wait()
        loads[3 + 2 * e].wait()
        p = lax.dot_general(ins[e], down_mat[...], (((1,), (1,)), ((), ())), preferred_element_type=F32)
        r = lax.dot_general(cots[e], up_mat[...], (((1,), (1,)), ((), ())), preferred_element_type=F32)
        both = jnp.concatenate([p, r, jnp.zeros((T, 128 - 2 * R), F32)], axis=1)
        both = jnp.concatenate([both, jnp.zeros((128 - T, 128), F32)], axis=0)
        both = both.T[: 2 * R]
        proj[:, 128 * e : 128 * (e + 1)] = both
        proj_in[x, :, 128 * e : 128 * (e + 1)] = both

    def send_x(low, high):
        lanes = slice(128 * low, 128 * high)
        pair = (proj.at[:, lanes], proj_in.at[x, :, lanes])
        wait_x.append(share([pair] * (NX - 1), to_x[1:], proj_in.at[: NX - 1, :, lanes]))

    held = [group for group in GROUPS if group[1] <= 3]
    for e in range(held[-1][1]):
        project(e)
    pl.semaphore_wait(barrier, len(greeted))
    for group in held:
        send_x(*group)
    for group in GROUPS[len(held) :]:
        for e in range(*group):
            project(e)
        send_x(*group)

    for load in small:
        load.wait()
    before = lax.broadcasted_iota(jnp.int32, (256, 256), 0)
    after = lax.broadcasted_iota(jnp.int32, (256, 256), 1)
    swap[...] = ((before % R == after // R) & (before // R == after % R)).astype(BF)

    token = lax.broadcasted_iota(jnp.int32, (2 * R, 128), 1)
    row = lax.broadcasted_iota(jnp.int32, (R, R), 0)
    col = lax.broadcasted_iota(jnp.int32, (R, R), 1)
    order = (col == 2 * (row % 8) + row // 8).astype(BF)
    lane = lax.broadcasted_iota(jnp.int32, (8, 128), 1)
    sub = lax.broadcasted_iota(jnp.int32, (8, 128), 0)
    norms = jnp.zeros((8, 128), F32)
    wait_d1, wait_u1, wait_d2, wait_u2 = [], [], [], []
    for (low, high), arrived in zip(GROUPS, wait_x):
        arrived()
        for e in range(low, high):
            lanes = slice(128 * e, 128 * (e + 1))
            total = proj_in[0, :, lanes] + proj_in[1, :, lanes] + proj_in[2, :, lanes] + proj_in[3, :, lanes]
            length = pub_len[0] if e == 0 else priv_len[e - 1]
            live = (total * (token < length).astype(F32)).astype(BF)
            pt = jnp.dot(order, live[:R], preferred_element_type=F32).astype(BF)
            rt = live[R:]
            gd = jnp.dot(rt[:, :T], ins[e], preferred_element_type=F32).astype(BF)
            for k in range(NY):
                d1s[k, R * e : R * (e + 1), :] = gd[:, 256 * k : 256 * (k + 1)]
            gu = jnp.dot(pt[:, :T], cots[e], preferred_element_type=F32).astype(BF).astype(F32)
            for k in range(NS):
                hi, lo = k // 8, k % 8
                rows = gu[8 * hi : 8 * hi + 8]
                pair = jnp.concatenate(
                    [rows[:, 256 * lo : 256 * lo + 128], rows[:, 256 * lo + 128 : 256 * lo + 256]], axis=0
                )
                u1s[k, R * e : R * (e + 1), :] = pair.astype(BF)
            if e:
                wide = gd.astype(F32)
                wide = wide * wide + gu * gu
                wide = tree([wide[:, 128 * k : 128 * (k + 1)] for k in range(16)])
                square = jnp.sum(jnp.sum(wide, axis=0, keepdims=True), axis=1, keepdims=True)
                here = (sub == (e - 1) * 2 + d // 64) & (lane == 64 + d % 64)
                norms = norms + jnp.where(here, square, 0.0)
        rows = slice(R * low, R * high)
        wait_d1.append(
            share(
                [(d1s.at[ys[k], rows], d1r.at[y, rows]) for k in range(1, NY)], to_y[1:], d1r.at[: NY - 1, rows]
            )
        )
        wait_u1.append(
            share(
                [(u1s.at[ss[k], rows], u1r.at[s, rows]) for k in range(1, NS)], to_s[1:], u1r.at[: NS - 1, rows]
            )
        )
        d1r[y, rows] = d1s[y, rows]
        u1r[s, rows] = u1s[s, rows]

    def flip(ref, e, h):
        cube = jnp.stack([ref[k, R * e : R * (e + 1), :].astype(F32)[8 * h : 8 * h + 8] for k in range(NS)], axis=0)
        return jnp.swapaxes(cube, 0, 1).astype(BF)

    def assemble(g):
        wait_d2[g]()
        wait_u2[g]()
        for e in range(*GROUPS[g]):
            for h in range(2):
                k = 2 * e + h
                rows = slice(128 * e, 128 * (e + 1))
                grads_ref[rows, 128 * h : 128 * (h + 1)] = flip(d2r, e, h).reshape(128, 128)
                grads_ref[rows, 256 + 128 * h : 256 + 128 * (h + 1)] = u2r[:, R * k : R * (k + 1), :].reshape(128, 128)

    def times_public(rows):
        return lax.dot_general(rows, grads_ref[:128], (((1,), (1,)), ((), ())), preferred_element_type=F32)

    def added(ref):
        n = ref.shape[0]
        return sum([ref[k] for k in range(1, n)], ref[0])

    def spread(src, dst, me, partners):
        dst[me] = src[...]
        return share([(src, dst.at[me])] * len(partners), partners, dst.at[: len(partners)])

    def relay(g):
        low, high = GROUPS[g]
        wait_d1[g]()
        for e in range(low, high):
            for hi in range(2):
                tiles = [d1r[k, R * e : R * (e + 1), 128 * hi : 128 * (hi + 1)].astype(F32) for k in range(NY)]
                halves = []
                for rh in range(2):
                    cube = jnp.stack([t[8 * rh : 8 * rh + 8] for t in tiles], axis=0)
                    cube = jnp.swapaxes(cube, 0, 1)
                    halves.append(lane_blocks([cube[i] for i in range(8)]))
                for lo in range(8):
                    pair = jnp.concatenate([halves[0][lo], halves[1][lo]], axis=0)
                    d2s[8 * hi + lo, R * e : R * (e + 1), :] = pair.astype(BF)
        rows = slice(R * low, R * high)
        wait_d2.append(
            share(
                [(d2s.at[ss[k], rows], d2r.at[s, rows]) for k in range(1, NS)], to_s[1:], d2r.at[: NS - 1, rows]
            )
        )
        d2r[s, rows] = d2s[s, rows]
        wait_u1[g]()
        for e in range(low, high):
            for h in range(2):
                k = 2 * e + h
                u2s[:, R * k : R * (k + 1), :] = flip(u1r, e, h)
        rows = slice(2 * R * low, 2 * R * high)
        wait_u2.append(
            share(
                [(u2s.at[ys[k], rows], u2r.at[y, rows]) for k in range(1, NY)], to_y[1:], u2r.at[: NY - 1, rows]
            )
        )
        u2r[y, rows] = u2s[y, rows]

    def send_gram():
        assemble(0)
        gram = times_public(grads_ref[:128])
        gm[...] = gram.reshape(16, 8, 128)
        gm[0] = jnp.where(lane >= 64, norms, gram[:8])
        gyr[q] = gm[q]
        return share([(gm.at[to], gyr.at[q]) for to in qs], to_q, gyr.at[: NS - 1])

    relay(0)
    relay(1)
    wait = send_gram()
    relay(2)
    wait()
    g2[...] = added(gyr)
    wait = spread(g2, gzr, z, to_z[1:])
    assemble(1)
    cm[0] = times_public(grads_ref[128:384]).reshape(2, 8, 16, 128)
    wait()
    g3[...] = added(gzr)
    wait = spread(g3, gxr, x, to_x[1:])
    assemble(2)
    cm[1] = times_public(grads_ref[384:640]).reshape(2, 8, 16, 128)
    wait_c = share([(cm.at[other], cmr)], [to_c], cmr)
    wait_c()
    c1[...] = cm[c] + cmr[...]
    car[y] = c1[0, y]
    wait_a = share([(c1.at[0, ys[k]], car.at[y]) for k in range(1, NY)], to_y[1:], car.at[: NY - 1])
    cbr[z] = c1[1, z]
    wait_b = share([(c1.at[1, zs[k]], cbr.at[z]) for k in range(1, NZ)], to_z[1:], cbr.at[: NZ - 1])
    wait()
    g4[...] = added(gxr)
    wait = spread(g4, gfull, q, to_q)
    wait()

    square = gfull[...].reshape(128, 128)
    down128 = lax.broadcasted_iota(jnp.int32, (128, 128), 0)
    over128 = lax.broadcasted_iota(jnp.int32, (128, 128), 1)
    gram = jnp.where(over128 > down128, square.T, square)
    diagonal = over128 == down128
    norm_scale = jnp.mean(
        jnp.sqrt(jnp.sum(jnp.where(diagonal, gram, 0.0), axis=0, keepdims=True)), axis=1, keepdims=True
    )
    coefficient_limit = CLIP_COEF * norm_scale
    residual_limit = CLIP_RESIDUAL * norm_scale
    unit = diagonal.astype(F32)
    blocks = [gram[8 * k : 8 * k + 8] for k in range(16)]
    units = [unit[8 * k : 8 * k + 8] for k in range(16)]
    early, blocks, units = inverse_factor(blocks, units, 0, SPLIT)
    wait_a()
    c2[0] = added(car)
    wait_a = spread(c2.at[0], caz, z, to_z[1:])
    wait_b()
    c2[1] = added(cbr)
    wait_b = spread(c2.at[1], cby, y, to_y[1:])
    late, _, _ = inverse_factor(blocks, units, SPLIT, 16)
    factor_inverse = jnp.concatenate(early + late, axis=0)
    wait_a()
    c3[0] = added(caz)
    wait_b()
    c3[1] = added(cby)
    wait = spread(c3, cxr, x, to_x[1:])
    wait()
    cross = added(cxr).reshape(32, 128)

    coeffs = lax.dot_general(
        cross, factor_inverse, (((1,), (1,)), ((), ())), preferred_element_type=F32, precision=PRECISE
    )
    coefficient_squares = jnp.sum(coeffs * coeffs, axis=1, keepdims=True)
    lane16 = lax.broadcasted_iota(jnp.int32, (16, 128), 1)
    sub16 = lax.broadcasted_iota(jnp.int32, (16, 128), 0)

    def own_squares(row, place):
        mine = jnp.sum(jnp.where(sub == row, square[:8], 0.0), axis=0, keepdims=True)
        return jnp.sum(jnp.where(lane16 == 64 + place * 16 + sub16, mine, 0.0), axis=1, keepdims=True)

    squares = jnp.concatenate(
        [own_squares(c * 4 + y // 4, y % 4), own_squares(c * 4 + 2 + z // 4, z % 4)], axis=0
    )
    residual_squares = jnp.maximum(squares - coefficient_squares, 0.0)
    keep_coefficient = coefficient_limit / jnp.maximum(jnp.sqrt(coefficient_squares), coefficient_limit)
    keep_residual = residual_limit / jnp.maximum(jnp.sqrt(residual_squares), residual_limit)
    weighted = coeffs * (keep_coefficient - keep_residual)

    def packed(part, place, row):
        correction = jnp.sum(weighted[part], axis=0, keepdims=True)
        keep = jnp.sum(jnp.where(lane16 == place * 16 + sub16, keep_residual[part], 0.0), axis=0, keepdims=True)
        return jnp.where(sub == 0, correction, jnp.where(sub == row, keep, 0.0))

    fa[...] = packed(slice(0, 16), y, 1 + 2 * c)
    wait_a = spread(fa, far, q, to_q)
    fb[...] = packed(slice(16, 32), z, 2 + 2 * c)
    wait_b = spread(fb, fbr, s, to_s[1:])
    wait_a()
    final = added(far)
    wait_b()
    final = final + added(fbr)
    target = jnp.sum(
        jnp.where(diagonal, final[0:1] + SIGMA_COEF * coefficient_limit * coef_noise[...], 0.0), axis=1, keepdims=True
    )
    anchor = jnp.sum(target * factor_inverse, axis=0, keepdims=True)
    weights = jnp.concatenate([anchor] + [final[k : k + 1] for k in range(1, E)], axis=1)
    update = exact_rows(weights, grads_ref[...])
    down = exact_rows(update[:, :256], swap[...])
    gain = 1.0 / math.sqrt(512 * T)
    out[0:1] = (down + SIGMA_RESIDUAL * residual_limit * down_noise[...]) * gain
    out[1:2] = (update[:, 256:] + SIGMA_RESIDUAL * residual_limit * up_noise[...]) * gain
    for copy in ends:
        copy.wait_send()


def parted_kernel(both, down_out, up_out):
    down_out[...] = both[0:1]
    up_out[...] = both[1:2]


def body(
    public_input_activations,
    public_output_cotangents,
    public_token_lengths,
    private_input_activations,
    private_output_cotangents,
    private_token_lengths,
    adapter_down_matrix,
    adapter_up_matrix,
    embedding_coefficient_noise,
    residual_down_noise,
    residual_up_noise,
):
    dma = pltpu.SemaphoreType.DMA
    v = pltpu.VMEM
    vm = pl.BlockSpec(memory_space=pltpu.VMEM)
    hbm = pl.BlockSpec(memory_space=pltpu.HBM)
    both = pl.pallas_call(
        body_kernel,
        out_shape=jax.ShapeDtypeStruct((2, 256), F32),
        in_specs=[hbm] * 11,
        out_specs=vm,
        scratch_shapes=[
            pltpu.SMEM((1,), jnp.int32), pltpu.SMEM((4,), jnp.int32), v((1, 128), F32), v((1, 256), F32), v((1, 256), F32),
            v((E, T, W), BF), v((E, T, W), BF), v((R, W), BF), v((R, W), BF), dma((12,)), dma((5,)),
            v((640, 512), BF), v((256, 256), BF),
            v((2 * R, 640), F32), v((NX, 2 * R, 640), F32),
            v((NY, 80, 256), BF), v((NY, 80, 256), BF),
            v((NS, 80, 128), BF), v((NS, 80, 128), BF),
            v((NS, 80, 128), BF), v((NS, 80, 128), BF),
            v((NY, 160, 128), BF), v((NY, 160, 128), BF),
            v((16, 8, 128), F32), v((NS, 8, 128), F32),
            v((8, 128), F32), v((NZ, 8, 128), F32), v((8, 128), F32), v((NX, 8, 128), F32), v((8, 128), F32),
            v((16, 8, 128), F32),
            v((2, 2, 8, 16, 128), F32), v((2, 8, 16, 128), F32), v((2, 8, 16, 128), F32),
            v((NY, 16, 128), F32), v((NZ, 16, 128), F32), v((2, 16, 128), F32),
            v((NZ, 16, 128), F32), v((NY, 16, 128), F32), v((2, 16, 128), F32), v((NX, 2, 16, 128), F32),
            v((8, 128), F32), v((NS, 8, 128), F32), v((8, 128), F32), v((NS, 8, 128), F32),
            dma((N_SHARES,)), dma((N_SHARES,)),
        ],
        compiler_params=pltpu.CompilerParams(collective_id=0, has_side_effects=True, vmem_limit_bytes=60 * 1024 * 1024),
    )(
        public_token_lengths, private_token_lengths,
        public_input_activations, public_output_cotangents,
        private_input_activations, private_output_cotangents,
        adapter_down_matrix.T, adapter_up_matrix,
        embedding_coefficient_noise[None], residual_down_noise, residual_up_noise,
    )
    return pl.pallas_call(
        parted_kernel,
        out_shape=(jax.ShapeDtypeStruct((1, 256), F32), jax.ShapeDtypeStruct((1, 256), F32)),
        in_specs=[vm],
        out_specs=(vm, vm),
    )(both)


def solution(mesh):
    placed = (
        P("dp", None, "mp"),
        P("dp", None, "mp"),
        P("dp"),
        P("dp", None, "mp"),
        P("dp", None, "mp"),
        P("dp"),
        P("mp", None),
        P(None, "mp"),
        P(),
        P("mp", "dp"),
        P("mp", "dp"),
    )
    return jax.shard_map(
        body, mesh=mesh, in_specs=placed, out_specs=(P("mp", "dp"), P("mp", "dp")), check_vma=False
    )
```

```python
import math

import jax
import jax.numpy as jnp
from jax import lax
from jax.experimental import pallas as pl
from jax.experimental.pallas import tpu as pltpu
from jax.sharding import PartitionSpec as P

CLIP_COEF = 0.5
CLIP_RESIDUAL = 0.7
SIGMA_COEF = 1.0
SIGMA_RESIDUAL = 0.04
PRECISE = lax.Precision.HIGHEST
BF, F32 = jnp.bfloat16, jnp.float32
NX, NY, NZ, NC = 4, 8, 8, 2
NS = NZ * NC
E = 5
SPLIT = 9
N_SHARES = 32
T = 112
GROUPS = ((0, 1), (1, 3), (3, 5))
W = 2048
R = 16
MESH = pl.DeviceIdType.MESH


def lane_blocks(rows):
    rows = list(rows)
    block = lax.broadcasted_iota(jnp.int32, rows[0].shape, rows[0].ndim - 1) // R
    axis = rows[0].ndim - 1
    for bit in (1, 2, 4):
        low = (block & bit) == 0
        fresh = list(rows)
        for i in range(8):
            if i & bit:
                continue
            j = i | bit
            fresh[i] = jnp.where(low, rows[i], pltpu.roll(rows[j], R * bit, axis))
            fresh[j] = jnp.where(low, pltpu.roll(rows[i], 128 - R * bit, axis), rows[j])
        rows = fresh
    return rows


def spread_lane(v, j):
    return jnp.broadcast_to(v[:, j : j + 1], v.shape)


def spread_row(v, i):
    return jnp.broadcast_to(v[i : i + 1], v.shape)


def tree(terms):
    terms = list(terms)
    while len(terms) > 1:
        terms = [sum(terms[i + 1 : i + 2], terms[i]) for i in range(0, len(terms), 2)]
    return terms[0]


def stacked(rows, sub):
    for bit in (1, 2, 4):
        odd = (sub & bit) != 0
        rows = [jnp.where(odd, rows[i + 1], rows[i]) for i in range(0, len(rows), 2)]
    return rows[0]


def inverse_factor(g, right, first, last):
    g, right = list(g), list(right)
    shape = (8, 128)
    sub = lax.broadcasted_iota(jnp.int32, shape, 0)
    zero = jnp.zeros(shape, F32)
    out = []
    for k in range(first, last):
        top, edge = g[k], right[k]
        cols = [spread_lane(top, 8 * k + j) for j in range(8)]
        a = {(i, j): spread_row(cols[j], i) for j in range(8) for i in range(j, 8)}
        inv = {}
        low = {}
        for j in range(8):
            p = a[j, j]
            r = lax.rsqrt(p)
            r = r * (1.5 - 0.5 * p * r * r)
            inv[j, j] = r
            for i in range(j + 1, 8):
                low[i, j] = a[i, j] * r
            for m in range(j + 1, 8):
                for i in range(m, 8):
                    a[i, m] = a[i, m] - low[i, j] * low[m, j]
            for i in range(j):
                inv[j, i] = -r * tree([low[j, m] * inv[m, i] for m in range(i, j)])
        top_rows = [spread_row(top, j) for j in range(8)]
        edge_rows = [spread_row(edge, j) for j in range(8)]
        inv_cols = [stacked([inv.get((i, j), zero) for i in range(8)], sub) for j in range(8)]
        edge = tree([inv_cols[j] * edge_rows[j] for j in range(8)])
        out.append(edge)
        if k == 15:
            break
        top = tree([inv_cols[j] * top_rows[j] for j in range(8)])
        top_rows = [spread_row(top, j) for j in range(8)]
        edge_rows = [spread_row(edge, j) for j in range(8)]
        turned = [stacked([inv.get((j, i), zero) for i in range(8)], sub) for j in range(8)]
        top = tree([turned[j] * top_rows[j] for j in range(8)])
        edge = tree([turned[j] * edge_rows[j] for j in range(8)])
        top_rows = [spread_row(top, j) for j in range(8)]
        edge_rows = [spread_row(edge, j) for j in range(8)]
        for m in range(k + 1, 16):
            factors = [spread_lane(g[m], 8 * k + j) for j in range(8)]
            g[m] = g[m] - tree([factors[j] * top_rows[j] for j in range(8)])
            right[m] = right[m] - tree([factors[j] * edge_rows[j] for j in range(8)])
    return out, g, right


def split(v):
    high = v.astype(BF)
    rest = v - high.astype(F32)
    middle = rest.astype(BF)
    return high, middle, (rest - middle.astype(F32)).astype(BF)


def exact_rows(row, matrix):
    terms = [t.astype(F32) for t in split(row)]
    terms = jnp.concatenate(terms + [jnp.zeros((5, row.shape[1]), F32)], axis=0).astype(BF)
    out = jnp.dot(terms, matrix, preferred_element_type=F32)
    return out[0:1] + out[1:2] + out[2:3]


def body_kernel(
    pub_len_hbm, priv_len_hbm, pub_in_hbm, pub_cot_hbm, priv_in_hbm, priv_cot_hbm, down_hbm, up_hbm,
    coef_hbm, down_noise_hbm, up_noise_hbm,
    out,
    pub_len, priv_len, coef_noise, down_noise, up_noise,
    ins, cots, down_mat, up_mat, load_sem, small_sem, grads_ref, swap,
    proj, proj_in, d1s, d1r, u1s, u1r, d2s, d2r, u2s, u2r,
    gm, gyr, g2, gzr, g3, gxr, g4, gfull,
    cm, cmr, c1, car, cbr, c2, caz, cby, c3, cxr, fa, far, fb, fbr,
    s_sem, r_sem,
):
    loads = [
        pltpu.make_async_copy(src, dst, load_sem.at[k])
        for k, (src, dst) in enumerate(
            [(down_hbm, down_mat), (up_hbm, up_mat), (pub_in_hbm.at[0], ins.at[0]), (pub_cot_hbm.at[0], cots.at[0])]
            + [
                pair
                for e in range(4)
                for pair in ((priv_in_hbm.at[e], ins.at[e + 1]), (priv_cot_hbm.at[e], cots.at[e + 1]))
            ]
        )
    ]
    small = [
        pltpu.make_async_copy(src, dst, small_sem.at[k])
        for k, (src, dst) in enumerate(
            [
                (pub_len_hbm, pub_len), (priv_len_hbm, priv_len),
                (coef_hbm, coef_noise), (down_noise_hbm, down_noise), (up_noise_hbm, up_noise),
            ]
        )
    ]
    for load in loads + small:
        load.start()
    x = lax.axis_index("mp")
    d = lax.axis_index("dp")
    y = d // NS
    s = d % NS
    z = s // NC
    c = s % NC

    def at(yy, ss, xx):
        return (yy * NS + ss, xx)

    xs = [lax.rem(x + k, NX) for k in range(NX)]
    ys = [lax.rem(y + k, NY) for k in range(NY)]
    ss = [lax.rem(s + k, NS) for k in range(NS)]
    zs = [lax.rem(z + k, NZ) for k in range(NZ)]
    to_x = [at(y, s, xs[k]) for k in range(NX)]
    to_y = [at(ys[k], s, x) for k in range(NY)]
    to_s = [at(y, ss[k], x) for k in range(NS)]
    to_z = [at(y, zs[k] * NC + c, x) for k in range(NZ)]
    other = 1 - c
    to_c = at(y, z * NC + other, x)
    q = y * NC + c
    turns = [(ky, kc) for ky in range(NY) for kc in range(NC)][1:]
    qs = [ys[ky] * NC + lax.rem(c + kc, NC) for ky, kc in turns]
    to_q = [at(ys[ky], z * NC + lax.rem(c + kc, NC), x) for ky, kc in turns]

    barrier = pltpu.get_barrier_semaphore()
    greeted = to_x[1:] + to_q[1:] + to_s[1:]
    for who in greeted:
        pl.semaphore_signal(barrier, inc=1, device_id=who, device_id_type=MESH)

    slots = []
    ends = []

    def remote(src, dst, k, who):
        return pltpu.make_async_remote_copy(
            src_ref=src, dst_ref=dst, send_sem=s_sem.at[k], recv_sem=r_sem.at[k], device_id=who, device_id_type=MESH
        )

    def share(pairs, partners, whole):
        k = len(slots)
        slots.append(k)
        for (src, dst), who in zip(pairs, partners):
            remote(src, dst, k, who).start()
        all_of = remote(whole, whole, k, partners[0])
        ends.append(all_of)
        return all_of.wait_recv

    loads[0].wait()
    loads[1].wait()
    wait_x = []

    def project(e):
        loads[2 + 2 * e].wait()
        loads[3 + 2 * e].wait()
        p = lax.dot_general(ins[e], down_mat[...], (((1,), (1,)), ((), ())), preferred_element_type=F32)
        r = lax.dot_general(cots[e], up_mat[...], (((1,), (1,)), ((), ())), preferred_element_type=F32)
        both = jnp.concatenate([p, r, jnp.zeros((T, 128 - 2 * R), F32)], axis=1)
        both = jnp.concatenate([both, jnp.zeros((128 - T, 128), F32)], axis=0)
        both = both.T[: 2 * R]
        proj[:, 128 * e : 128 * (e + 1)] = both
        proj_in[x, :, 128 * e : 128 * (e + 1)] = both

    def send_x(low, high):
        lanes = slice(128 * low, 128 * high)
        pair = (proj.at[:, lanes], proj_in.at[x, :, lanes])
        wait_x.append(share([pair] * (NX - 1), to_x[1:], proj_in.at[: NX - 1, :, lanes]))

    held = [group for group in GROUPS if group[1] <= 3]
    for e in range(held[-1][1]):
        project(e)
    pl.semaphore_wait(barrier, len(greeted))
    for group in held:
        send_x(*group)
    for group in GROUPS[len(held) :]:
        for e in range(*group):
            project(e)
        send_x(*group)

    for load in small:
        load.wait()
    before = lax.broadcasted_iota(jnp.int32, (256, 256), 0)
    after = lax.broadcasted_iota(jnp.int32, (256, 256), 1)
    swap[...] = ((before % R == after // R) & (before // R == after % R)).astype(BF)

    token = lax.broadcasted_iota(jnp.int32, (2 * R, 128), 1)
    row = lax.broadcasted_iota(jnp.int32, (R, R), 0)
    col = lax.broadcasted_iota(jnp.int32, (R, R), 1)
    order = (col == 2 * (row % 8) + row // 8).astype(BF)
    lane = lax.broadcasted_iota(jnp.int32, (8, 128), 1)
    sub = lax.broadcasted_iota(jnp.int32, (8, 128), 0)
    norms = jnp.zeros((8, 128), F32)
    wait_d1, wait_u1, wait_d2, wait_u2 = [], [], [], []
    for (low, high), arrived in zip(GROUPS, wait_x):
        arrived()
        for e in range(low, high):
            lanes = slice(128 * e, 128 * (e + 1))
            total = proj_in[0, :, lanes] + proj_in[1, :, lanes] + proj_in[2, :, lanes] + proj_in[3, :, lanes]
            length = pub_len[0] if e == 0 else priv_len[e - 1]
            live = (total * (token < length).astype(F32)).astype(BF)
            pt = jnp.dot(order, live[:R], preferred_element_type=F32).astype(BF)
            rt = live[R:]
            gd = jnp.dot(rt[:, :T], ins[e], preferred_element_type=F32).astype(BF)
            for k in range(NY):
                d1s[k, R * e : R * (e + 1), :] = gd[:, 256 * k : 256 * (k + 1)]
            gu = jnp.dot(pt[:, :T], cots[e], preferred_element_type=F32).astype(BF).astype(F32)
            for k in range(NS):
                hi, lo = k // 8, k % 8
                rows = gu[8 * hi : 8 * hi + 8]
                pair = jnp.concatenate(
                    [rows[:, 256 * lo : 256 * lo + 128], rows[:, 256 * lo + 128 : 256 * lo + 256]], axis=0
                )
                u1s[k, R * e : R * (e + 1), :] = pair.astype(BF)
            if e:
                wide = gd.astype(F32)
                wide = wide * wide + gu * gu
                wide = tree([wide[:, 128 * k : 128 * (k + 1)] for k in range(16)])
                square = jnp.sum(jnp.sum(wide, axis=0, keepdims=True), axis=1, keepdims=True)
                here = (sub == (e - 1) * 2 + d // 64) & (lane == 64 + d % 64)
                norms = norms + jnp.where(here, square, 0.0)
        rows = slice(R * low, R * high)
        wait_d1.append(
            share(
                [(d1s.at[ys[k], rows], d1r.at[y, rows]) for k in range(1, NY)], to_y[1:], d1r.at[: NY - 1, rows]
            )
        )
        wait_u1.append(
            share(
                [(u1s.at[ss[k], rows], u1r.at[s, rows]) for k in range(1, NS)], to_s[1:], u1r.at[: NS - 1, rows]
            )
        )
        d1r[y, rows] = d1s[y, rows]
        u1r[s, rows] = u1s[s, rows]

    def flip(ref, e, h):
        cube = jnp.stack([ref[k, R * e : R * (e + 1), :].astype(F32)[8 * h : 8 * h + 8] for k in range(NS)], axis=0)
        return jnp.swapaxes(cube, 0, 1).astype(BF)

    def assemble(g):
        wait_d2[g]()
        wait_u2[g]()
        for e in range(*GROUPS[g]):
            for h in range(2):
                k = 2 * e + h
                rows = slice(128 * e, 128 * (e + 1))
                grads_ref[rows, 128 * h : 128 * (h + 1)] = flip(d2r, e, h).reshape(128, 128)
                grads_ref[rows, 256 + 128 * h : 256 + 128 * (h + 1)] = u2r[:, R * k : R * (k + 1), :].reshape(128, 128)

    def times_public(rows):
        return lax.dot_general(rows, grads_ref[:128], (((1,), (1,)), ((), ())), preferred_element_type=F32)

    def added(ref):
        n = ref.shape[0]
        return sum([ref[k] for k in range(1, n)], ref[0])

    def spread(src, dst, me, partners):
        dst[me] = src[...]
        return share([(src, dst.at[me])] * len(partners), partners, dst.at[: len(partners)])

    def relay(g):
        low, high = GROUPS[g]
        wait_d1[g]()
        for e in range(low, high):
            for hi in range(2):
                tiles = [d1r[k, R * e : R * (e + 1), 128 * hi : 128 * (hi + 1)].astype(F32) for k in range(NY)]
                halves = []
                for rh in range(2):
                    cube = jnp.stack([t[8 * rh : 8 * rh + 8] for t in tiles], axis=0)
                    cube = jnp.swapaxes(cube, 0, 1)
                    halves.append(lane_blocks([cube[i] for i in range(8)]))
                for lo in range(8):
                    pair = jnp.concatenate([halves[0][lo], halves[1][lo]], axis=0)
                    d2s[8 * hi + lo, R * e : R * (e + 1), :] = pair.astype(BF)
        rows = slice(R * low, R * high)
        wait_d2.append(
            share(
                [(d2s.at[ss[k], rows], d2r.at[s, rows]) for k in range(1, NS)], to_s[1:], d2r.at[: NS - 1, rows]
            )
        )
        d2r[s, rows] = d2s[s, rows]
        wait_u1[g]()
        for e in range(low, high):
            for h in range(2):
                k = 2 * e + h
                u2s[:, R * k : R * (k + 1), :] = flip(u1r, e, h)
        rows = slice(2 * R * low, 2 * R * high)
        wait_u2.append(
            share(
                [(u2s.at[ys[k], rows], u2r.at[y, rows]) for k in range(1, NY)], to_y[1:], u2r.at[: NY - 1, rows]
            )
        )
        u2r[y, rows] = u2s[y, rows]

    def send_gram():
        assemble(0)
        gram = times_public(grads_ref[:128])
        gm[...] = gram.reshape(16, 8, 128)
        gm[0] = jnp.where(lane >= 64, norms, gram[:8])
        gyr[q] = gm[q]
        return share([(gm.at[to], gyr.at[q]) for to in qs], to_q, gyr.at[: NS - 1])

    relay(0)
    relay(1)
    wait = send_gram()
    relay(2)
    assemble(1)
    cm[0] = times_public(grads_ref[128:384]).reshape(2, 8, 16, 128)
    wait()
    g2[...] = added(gyr)
    wait = spread(g2, gzr, z, to_z[1:])
    assemble(2)
    cm[1] = times_public(grads_ref[384:640]).reshape(2, 8, 16, 128)
    wait_c = share([(cm.at[other], cmr)], [to_c], cmr)
    wait()
    g3[...] = added(gzr)
    wait = spread(g3, gxr, x, to_x[1:])
    wait_c()
    c1[...] = cm[c] + cmr[...]
    car[y] = c1[0, y]
    wait_a = share([(c1.at[0, ys[k]], car.at[y]) for k in range(1, NY)], to_y[1:], car.at[: NY - 1])
    cbr[z] = c1[1, z]
    wait_b = share([(c1.at[1, zs[k]], cbr.at[z]) for k in range(1, NZ)], to_z[1:], cbr.at[: NZ - 1])
    wait()
    g4[...] = added(gxr)
    wait = spread(g4, gfull, q, to_q)
    wait_a()
    c2[0] = added(car)
    wait_a = spread(c2.at[0], caz, z, to_z[1:])
    wait_b()
    c2[1] = added(cbr)
    wait_b = spread(c2.at[1], cby, y, to_y[1:])
    wait()

    square = gfull[...].reshape(128, 128)
    down128 = lax.broadcasted_iota(jnp.int32, (128, 128), 0)
    over128 = lax.broadcasted_iota(jnp.int32, (128, 128), 1)
    gram = jnp.where(over128 > down128, square.T, square)
    diagonal = over128 == down128
    norm_scale = jnp.mean(
        jnp.sqrt(jnp.sum(jnp.where(diagonal, gram, 0.0), axis=0, keepdims=True)), axis=1, keepdims=True
    )
    coefficient_limit = CLIP_COEF * norm_scale
    residual_limit = CLIP_RESIDUAL * norm_scale
    unit = diagonal.astype(F32)
    blocks = [gram[8 * k : 8 * k + 8] for k in range(16)]
    units = [unit[8 * k : 8 * k + 8] for k in range(16)]
    early, blocks, units = inverse_factor(blocks, units, 0, SPLIT)
    wait_a()
    c3[0] = added(caz)
    wait_b()
    c3[1] = added(cby)
    wait = spread(c3, cxr, x, to_x[1:])
    late, _, _ = inverse_factor(blocks, units, SPLIT, 16)
    factor_inverse = jnp.concatenate(early + late, axis=0)
    wait()
    cross = added(cxr).reshape(32, 128)

    coeffs = lax.dot_general(
        cross, factor_inverse, (((1,), (1,)), ((), ())), preferred_element_type=F32, precision=PRECISE
    )
    coefficient_squares = jnp.sum(coeffs * coeffs, axis=1, keepdims=True)
    lane16 = lax.broadcasted_iota(jnp.int32, (16, 128), 1)
    sub16 = lax.broadcasted_iota(jnp.int32, (16, 128), 0)

    def own_squares(row, place):
        mine = jnp.sum(jnp.where(sub == row, square[:8], 0.0), axis=0, keepdims=True)
        return jnp.sum(jnp.where(lane16 == 64 + place * 16 + sub16, mine, 0.0), axis=1, keepdims=True)

    squares = jnp.concatenate(
        [own_squares(c * 4 + y // 4, y % 4), own_squares(c * 4 + 2 + z // 4, z % 4)], axis=0
    )
    residual_squares = jnp.maximum(squares - coefficient_squares, 0.0)
    keep_coefficient = coefficient_limit / jnp.maximum(jnp.sqrt(coefficient_squares), coefficient_limit)
    keep_residual = residual_limit / jnp.maximum(jnp.sqrt(residual_squares), residual_limit)
    weighted = coeffs * (keep_coefficient - keep_residual)

    def packed(part, place, row):
        correction = jnp.sum(weighted[part], axis=0, keepdims=True)
        keep = jnp.sum(jnp.where(lane16 == place * 16 + sub16, keep_residual[part], 0.0), axis=0, keepdims=True)
        return jnp.where(sub == 0, correction, jnp.where(sub == row, keep, 0.0))

    fa[...] = packed(slice(0, 16), y, 1 + 2 * c)
    wait_a = spread(fa, far, q, to_q)
    fb[...] = packed(slice(16, 32), z, 2 + 2 * c)
    wait_b = spread(fb, fbr, s, to_s[1:])
    wait_a()
    final = added(far)
    wait_b()
    final = final + added(fbr)
    target = jnp.sum(
        jnp.where(diagonal, final[0:1] + SIGMA_COEF * coefficient_limit * coef_noise[...], 0.0), axis=1, keepdims=True
    )
    anchor = jnp.sum(target * factor_inverse, axis=0, keepdims=True)
    weights = jnp.concatenate([anchor] + [final[k : k + 1] for k in range(1, E)], axis=1)
    update = exact_rows(weights, grads_ref[...])
    down = exact_rows(update[:, :256], swap[...])
    gain = 1.0 / math.sqrt(512 * T)
    out[0:1] = (down + SIGMA_RESIDUAL * residual_limit * down_noise[...]) * gain
    out[1:2] = (update[:, 256:] + SIGMA_RESIDUAL * residual_limit * up_noise[...]) * gain
    for copy in ends:
        copy.wait_send()


def parted_kernel(both, down_out, up_out):
    down_out[...] = both[0:1]
    up_out[...] = both[1:2]


def body(
    public_input_activations,
    public_output_cotangents,
    public_token_lengths,
    private_input_activations,
    private_output_cotangents,
    private_token_lengths,
    adapter_down_matrix,
    adapter_up_matrix,
    embedding_coefficient_noise,
    residual_down_noise,
    residual_up_noise,
):
    dma = pltpu.SemaphoreType.DMA
    v = pltpu.VMEM
    vm = pl.BlockSpec(memory_space=pltpu.VMEM)
    hbm = pl.BlockSpec(memory_space=pltpu.HBM)
    both = pl.pallas_call(
        body_kernel,
        out_shape=jax.ShapeDtypeStruct((2, 256), F32),
        in_specs=[hbm] * 11,
        out_specs=vm,
        scratch_shapes=[
            pltpu.SMEM((1,), jnp.int32), pltpu.SMEM((4,), jnp.int32), v((1, 128), F32), v((1, 256), F32), v((1, 256), F32),
            v((E, T, W), BF), v((E, T, W), BF), v((R, W), BF), v((R, W), BF), dma((12,)), dma((5,)),
            v((640, 512), BF), v((256, 256), BF),
            v((2 * R, 640), F32), v((NX, 2 * R, 640), F32),
            v((NY, 80, 256), BF), v((NY, 80, 256), BF),
            v((NS, 80, 128), BF), v((NS, 80, 128), BF),
            v((NS, 80, 128), BF), v((NS, 80, 128), BF),
            v((NY, 160, 128), BF), v((NY, 160, 128), BF),
            v((16, 8, 128), F32), v((NS, 8, 128), F32),
            v((8, 128), F32), v((NZ, 8, 128), F32), v((8, 128), F32), v((NX, 8, 128), F32), v((8, 128), F32),
            v((16, 8, 128), F32),
            v((2, 2, 8, 16, 128), F32), v((2, 8, 16, 128), F32), v((2, 8, 16, 128), F32),
            v((NY, 16, 128), F32), v((NZ, 16, 128), F32), v((2, 16, 128), F32),
            v((NZ, 16, 128), F32), v((NY, 16, 128), F32), v((2, 16, 128), F32), v((NX, 2, 16, 128), F32),
            v((8, 128), F32), v((NS, 8, 128), F32), v((8, 128), F32), v((NS, 8, 128), F32),
            dma((N_SHARES,)), dma((N_SHARES,)),
        ],
        compiler_params=pltpu.CompilerParams(collective_id=0, has_side_effects=True, vmem_limit_bytes=60 * 1024 * 1024),
    )(
        public_token_lengths, private_token_lengths,
        public_input_activations, public_output_cotangents,
        private_input_activations, private_output_cotangents,
        adapter_down_matrix.T, adapter_up_matrix,
        embedding_coefficient_noise[None], residual_down_noise, residual_up_noise,
    )
    return pl.pallas_call(
        parted_kernel,
        out_shape=(jax.ShapeDtypeStruct((1, 256), F32), jax.ShapeDtypeStruct((1, 256), F32)),
        in_specs=[vm],
        out_specs=(vm, vm),
    )(both)


def solution(mesh):
    placed = (
        P("dp", None, "mp"),
        P("dp", None, "mp"),
        P("dp"),
        P("dp", None, "mp"),
        P("dp", None, "mp"),
        P("dp"),
        P("mp", None),
        P(None, "mp"),
        P(),
        P("mp", "dp"),
        P("mp", "dp"),
    )
    return jax.shard_map(
        body, mesh=mesh, in_specs=placed, out_specs=(P("mp", "dp"), P("mp", "dp")), check_vma=False
    )
```
